32 devices in a mesh: pool: 8 (over y, x, core), mp: 4 (over z).
Axes of the slice: x: 2, y: 2, z: 4, core: 2. Of those that a mesh axis runs over, the one named last changes fastest.
Arguments:
- hidden_in: bfloat16 [32, 2048], P('pool')
- mix_gain: float32 [2048], replicated, may hold values from 0.25 to 1.75
- project_in: bfloat16 [2048, 1920], P(None, 'mp'), may hold values from -0.125 to 0.125
- query_gain: float32 [64], replicated, may hold values from 0.1 to 1.9
- key_gain: float32 [64], replicated, may hold values from 0.1 to 1.9
- page_cache: bfloat16 [512, 128, 640], P(('pool', 'mp')), may hold values from -2.5 to 2.5
- page_table: int32 [32, 64], replicated, may hold values from -1 to 511, as said below
- lengths: int32 [32], replicated, may hold values from 1 to 8192, as said below
- row_order: int32 [32], replicated, may hold values from 0 to 31, each once
- out_weight: bfloat16 [1280, 2048], P('mp'), may hold values from -0.75 to 0.75
- feed_gain: float32 [2048], replicated, may hold values from 0.25 to 1.75
- gate_weight: bfloat16 [2048, 5120], P(None, 'mp'), may hold values from -0.125 to 0.125
- up_weight: bfloat16 [2048, 5120], P(None, 'mp'), may hold values from -0.125 to 0.125
- down_weight: bfloat16 [5120, 2048], P('mp'), may hold values from -0.078125 to 0.078125
Outputs:
- hidden_out: bfloat16 [32, 2048], P(('pool', 'mp'))
- new_entries: bfloat16 [32, 640], P(('pool', 'mp'))
The draws below stay inside these ranges and needn't reach their ends.
Inputs may be any that keep to these rules, and one draw needn't show every extreme that they name: Request r has lengths[r] cached tokens; one request in every draw has exactly 8192. `page_table`: entries j of request r with j * 128 < lengths[r] hold page numbers, no page appearing twice in the table; all other entries are -1. Row i of hidden_in serves request row_order[i].
All inputs are finite; a program needn't handle non-finite values.
Results may differ from the reference program's by a relative error of at most 0.014.
Values may be sent and summed in bfloat16 or wider, within the bound.
No kernel may reach another device: no remote copies, remote signals or barrier semaphores. Data moves between devices by JAX's collectives and lax.ppermute only.
A program may use at most 64 MiB of HBM per device.

```python
import math
import jax
import jax.numpy as jnp
from jax import lax

D = 2048
H = 20
KVH = 5
HD = 64
FF = 5120
PAGE = 128
MAXLEN = 8192
MAXP = 64
R = 32
PAGES = 512
QKVW = 1920
KVW = 640


def draw_hidden_in(key, part):
    folded = jax.random.fold_in(key, 11)
    key_entries, key_rows, key_columns = jax.random.split(folded, 3)
    entries = jnp.clip(jax.random.normal(key_entries, (R, D), jnp.float32), -4.0, 4.0)
    row_scale = jnp.exp(jax.random.uniform(key_rows, (R, 1), jnp.float32, math.log(0.1), math.log(1.0)))
    column_scale = jnp.exp(jax.random.uniform(key_columns, (1, D), jnp.float32, math.log(0.3), math.log(3.0)))
    return (entries * row_scale * column_scale).astype(jnp.bfloat16)


def request_layout(key):
    folded = jax.random.fold_in(key, 23)
    key_weight, key_pick, key_shuffle = jax.random.split(folded, 3)
    exponents = jax.random.randint(key_weight, (R,), 0, 9)
    weights = jnp.left_shift(jnp.ones((R,), jnp.int32), exponents.astype(jnp.int32))
    budget = PAGE * (PAGES - 2 * R - MAXP)
    weight_sum = jnp.sum(weights)
    quotient = budget // weight_sum
    remainder = budget % weight_sum
    lengths = 1 + quotient * weights + remainder * weights // weight_sum
    lengths = jnp.minimum(lengths, MAXLEN)
    longest = jax.random.randint(key_pick, (), 0, R)
    lengths = jnp.where(jnp.arange(R) == longest, MAXLEN, lengths).astype(jnp.int32)
    page_counts = (lengths + PAGE - 1) // PAGE
    offsets = jnp.cumsum(page_counts) - page_counts
    shuffled = jax.random.permutation(key_shuffle, PAGES).astype(jnp.int32)
    shuffled = (shuffled + (PAGES - 1 - shuffled[0])) % PAGES
    columns = jnp.arange(MAXP, dtype=jnp.int32)
    slot_index = jnp.clip(offsets[:, None] + columns[None, :], 0, PAGES - 1)
    page_map = jnp.where(columns[None, :] < page_counts[:, None], shuffled[slot_index], -1).astype(jnp.int32)
    return (lengths, page_map)


def draw_lengths(key, part):
    return request_layout(key)[0]


def draw_page_table(key, part):
    return request_layout(key)[1]


def block_scale(stream_key, dims, shards, smallest, high):
    factor_of, own = 1.0, jax.random.fold_in(stream_key, 6)
    for axis_at, parts in shards:
        steps = jnp.exp(jax.random.uniform(jax.random.fold_in(own, axis_at), (parts,), jnp.float32, smallest / len(shards), high / len(shards)))
        factor_of = factor_of * jnp.repeat(steps, dims[axis_at] // parts).reshape([-1 if axis == axis_at else 1 for axis in range(len(dims))])
    return factor_of


def gaussian(rng, extent, deviation, limit, cuts=(), kind=jnp.bfloat16):
    values = jax.random.normal(rng, extent, jnp.float32) * deviation
    if len(cuts) > 0:
        values = block_scale(rng, extent, cuts, -0.22, 0.18) * values
    return jnp.clip(values, min=-limit, max=limit).astype(kind)


def setup_inputs(seed: int = 0) -> dict:
    streams_of = jax.random.split(jax.random.key(seed), 15)
    return {
        "hidden_in": draw_hidden_in(jax.random.fold_in(streams_of[14], 71), 0),
        "mix_gain": jnp.clip(1.0 + 0.15 * jax.random.normal(streams_of[1], (D,), jnp.float32), 0.25, 1.75),
        "project_in": gaussian(streams_of[2], (D, QKVW), D ** -0.5, 0.125, ((1, 4),)),
        "query_gain": jnp.clip(1.0 + 0.18 * jax.random.normal(streams_of[3], (HD,), jnp.float32), 0.1, 1.9),
        "key_gain": jnp.clip(1.0 + 0.18 * jax.random.normal(streams_of[4], (HD,), jnp.float32), 0.1, 1.9),
        "page_cache": jnp.clip(jax.random.uniform(streams_of[5], (PAGES, PAGE, KVW), jnp.float32, -2.5, 2.5) * block_scale(streams_of[5], (PAGES, PAGE, KVW), ((0, 32),), -0.4, 0.0), -2.5, 2.5).astype(jnp.bfloat16),
        "page_table": draw_page_table(jax.random.fold_in(streams_of[14], 71), 0),
        "lengths": draw_lengths(jax.random.fold_in(streams_of[14], 71), 0),
        "row_order": jax.random.permutation(streams_of[8], R).astype(jnp.int32),
        "out_weight": gaussian(streams_of[9], (H * HD, D), HD ** -0.5, 0.75, ((0, 4),)),
        "feed_gain": jnp.clip(1.0 + 0.15 * jax.random.normal(streams_of[10], (D,), jnp.float32), 0.25, 1.75),
        "gate_weight": gaussian(streams_of[11], (D, FF), D ** -0.5, 0.125, ((1, 4),)),
        "up_weight": gaussian(streams_of[12], (D, FF), D ** -0.5, 0.125, ((1, 4),)),
        "down_weight": gaussian(streams_of[13], (FF, D), FF ** -0.5, 0.078125, ((0, 4),)),
    }


EPS_WIDE = 1e-05
EPS_HEAD = 1e-06

def rms_scale(values, scaling, epsilon):
    mean_square = lax.optimization_barrier(jnp.mean(values * values, axis=-1, keepdims=True))
    return values * lax.rsqrt(mean_square + epsilon) * scaling

def rotate(head_rows, positions):
    middle = head_rows.shape[-1] // 2
    frequency = 10000.0 ** (-(2.0 * jnp.arange(middle, dtype=jnp.float32)) / head_rows.shape[-1])
    angles = positions.astype(jnp.float32)[..., None, None] * frequency
    cosines = jnp.cos(angles)
    sine_term = jnp.sin(angles)
    low_half = head_rows[..., :middle]
    high_half = head_rows[..., middle:]
    return jnp.concatenate([low_half * cosines - high_half * sine_term, high_half * cosines + low_half * sine_term], axis=-1)

def reference(hidden_in, mix_gain, project_in, query_gain, key_gain, page_cache, page_table, lengths, row_order, out_weight, feed_gain, gate_weight, up_weight, down_weight):
    inv_root = HD ** (-0.5)
    groups = H // KVH
    wide_rows = hidden_in.astype(jnp.float32)
    normed = rms_scale(wide_rows, mix_gain, EPS_WIDE).astype(jnp.bfloat16)
    packed = jnp.dot(normed, project_in, preferred_element_type=jnp.float32).astype(jnp.bfloat16)
    row_lengths = lengths[row_order]
    row_tables = page_table[row_order]
    queries = packed[:, :H * HD].astype(jnp.float32).reshape(R, H, HD)
    key_new = packed[:, H * HD:(H + KVH) * HD].astype(jnp.float32).reshape(R, KVH, HD)
    value_new = packed[:, (H + KVH) * HD:]
    queries = rotate(rms_scale(queries, query_gain, EPS_HEAD), row_lengths).astype(jnp.bfloat16)
    key_new = rotate(rms_scale(key_new, key_gain, EPS_HEAD), row_lengths).astype(jnp.bfloat16)
    new_entries = jnp.concatenate([key_new.reshape(R, KVH * HD), value_new], axis=1)

    def attend_one(items):
        query_row, key_row, value_row, table_row, length = items
        page_rows = page_cache[jnp.clip(table_row, 0, PAGES - 1)].reshape(MAXP * PAGE, 2 * KVH * HD)
        key_rows = page_rows[:, :KVH * HD].astype(jnp.float32).reshape(MAXP * PAGE, KVH, HD)
        value_rows = page_rows[:, KVH * HD:].astype(jnp.float32).reshape(MAXP * PAGE, KVH, HD)
        grouped = query_row.astype(jnp.float32).reshape(KVH, groups, HD)
        scores = jnp.einsum('kgd,tkd->kgt', grouped, key_rows) * inv_root
        in_range = jnp.arange(MAXP * PAGE) < length
        weights = jnp.where(in_range, jnp.exp(scores), 0.0)
        own_score = jnp.einsum('kgd,kd->kg', grouped, key_row.astype(jnp.float32)) * inv_root
        own_weight = jnp.exp(own_score)
        denominator = lax.optimization_barrier(jnp.sum(weights, axis=-1)) + own_weight
        rounded = lax.optimization_barrier(weights.astype(jnp.bfloat16)).astype(jnp.float32)
        own_rounded = lax.optimization_barrier(own_weight.astype(jnp.bfloat16)).astype(jnp.float32)
        numerator = jnp.einsum('kgt,tkd->kgd', rounded, value_rows)
        numerator = numerator + own_rounded[..., None] * value_row.astype(jnp.float32).reshape(KVH, 1, HD)
        return (numerator / denominator[..., None]).reshape(H * HD).astype(jnp.bfloat16)
    attended = lax.map(attend_one, (queries, key_new, value_new, row_tables, row_lengths))
    projected = jnp.dot(attended, out_weight, preferred_element_type=jnp.float32)
    mixed_rows = (wide_rows + projected).astype(jnp.bfloat16)
    normed_two = rms_scale(mixed_rows.astype(jnp.float32), feed_gain, EPS_WIDE).astype(jnp.bfloat16)
    gate_values = jnp.dot(normed_two, gate_weight, preferred_element_type=jnp.float32)
    up_values = jnp.dot(normed_two, up_weight, preferred_element_type=jnp.float32)
    hidden = (jax.nn.silu(gate_values) * up_values).astype(jnp.bfloat16)
    hidden_out = (mixed_rows.astype(jnp.float32) + jnp.dot(hidden, down_weight, preferred_element_type=jnp.float32)).astype(jnp.bfloat16)
    return (hidden_out, new_entries)
```

```python
import jax
import jax.numpy as jnp
from jax import lax
from jax.sharding import PartitionSpec as P

H = 20
KVH = 5
HD = 64
PAGE = 128
MAXP = 64


EPS_WIDE = 1e-05
EPS_HEAD = 1e-06


def rms_scale(values, scaling, epsilon):
    mean_square = jnp.mean(values * values, axis=-1, keepdims=True)
    return values * lax.rsqrt(mean_square + epsilon) * scaling


def rotate(head_rows, positions):
    middle = head_rows.shape[-1] // 2
    frequency = 10000.0 ** (-(2.0 * jnp.arange(middle, dtype=jnp.float32)) / head_rows.shape[-1])
    angles = positions.astype(jnp.float32)[..., None, None] * frequency
    cosines = jnp.cos(angles)
    sine_term = jnp.sin(angles)
    low_half = head_rows[..., :middle]
    high_half = head_rows[..., middle:]
    return jnp.concatenate(
        [low_half * cosines - high_half * sine_term, high_half * cosines + low_half * sine_term],
        axis=-1,
    )


def shards(
    hidden_in,
    mix_gain,
    project_in,
    query_gain,
    key_gain,
    page_cache,
    page_table,
    lengths,
    row_order,
    out_weight,
    feed_gain,
    gate_weight,
    up_weight,
    down_weight,
):
    pool_count = lax.axis_size("pool")
    mp_count = lax.axis_size("mp")
    pool_index = lax.axis_index("pool")
    mp_index = lax.axis_index("mp")
    group_rows = hidden_in.shape[0]
    local_pages = page_cache.shape[0]
    head_cols = H * HD // mp_count
    groups = H // KVH
    inv_root = HD ** (-0.5)
    highest = lax.Precision.HIGHEST
    wide_rows = hidden_in.astype(jnp.float32)
    normed = rms_scale(wide_rows, mix_gain, EPS_WIDE).astype(jnp.bfloat16)
    packed_part = jnp.dot(normed, project_in, preferred_element_type=jnp.float32).astype(
        jnp.bfloat16
    )
    device_count = pool_count * mp_count
    gathered = lax.all_to_all(
        jnp.broadcast_to(packed_part[None], (device_count,) + packed_part.shape),
        ("pool", "mp"),
        0,
        0,
        tiled=True,
    )
    packed = (
        gathered.reshape(pool_count, mp_count, group_rows, -1)
        .transpose(2, 0, 1, 3)
        .reshape(group_rows, pool_count, (H + 2 * KVH) * HD)
    )
    request_ids = row_order.reshape(pool_count, group_rows).T
    row_lengths = lengths[request_ids]
    row_tables = page_table[request_ids]
    queries = packed[..., : H * HD].astype(jnp.float32).reshape(group_rows, pool_count, H, HD)
    queries = rotate(rms_scale(queries, query_gain, EPS_HEAD), row_lengths).astype(jnp.bfloat16)
    own_packed = lax.dynamic_index_in_dim(packed, pool_index, 1, keepdims=False)
    own_lengths = lax.dynamic_index_in_dim(row_lengths, pool_index, 1, keepdims=False)
    own_queries = lax.dynamic_index_in_dim(queries, pool_index, 1, keepdims=False)
    key_new = (
        own_packed[:, H * HD : (H + KVH) * HD].astype(jnp.float32).reshape(group_rows, KVH, HD)
    )
    key_new = rotate(rms_scale(key_new, key_gain, EPS_HEAD), own_lengths).astype(jnp.bfloat16)
    value_new = own_packed[:, (H + KVH) * HD :].reshape(group_rows, KVH, HD)
    own_score = (
        jnp.einsum(
            "qkgd,qkd->qkg",
            own_queries.reshape(group_rows, KVH, groups, HD),
            key_new,
            preferred_element_type=jnp.float32,
        )
        * inv_root
    )
    own_weight = jnp.exp(own_score)
    own_numerator = jnp.einsum(
        "qkg,qkd->qkgd",
        own_weight.astype(jnp.bfloat16),
        value_new,
        preferred_element_type=jnp.float32,
    ).reshape(group_rows, H * HD)
    own_weight = own_weight.reshape(group_rows, H)
    page_ids = (pool_index * mp_count + mp_index) * local_pages + jnp.arange(
        local_pages, dtype=jnp.int32
    )
    matches = row_tables[None] == page_ids[:, None, None, None]
    chosen = jnp.any(matches, axis=-1)
    blocks = jnp.sum(jnp.where(matches, jnp.arange(MAXP, dtype=jnp.int32), 0), axis=(1, 2, 3))
    page_length = jnp.sum(jnp.where(chosen, row_lengths[None], 0), axis=(1, 2))
    chosen_half = chosen.astype(jnp.bfloat16)
    chosen_full = chosen.astype(jnp.float32)
    page_queries = jnp.einsum(
        "sqp,qphd->shd", chosen_half, queries, preferred_element_type=jnp.float32
    ).astype(jnp.bfloat16)
    key_rows = page_cache[..., : KVH * HD].reshape(local_pages, PAGE, KVH, HD)
    value_rows = page_cache[..., KVH * HD :].reshape(local_pages, PAGE, KVH, HD)
    scores = (
        jnp.einsum(
            "skgd,stkd->skgt",
            page_queries.reshape(local_pages, KVH, groups, HD),
            key_rows,
            preferred_element_type=jnp.float32,
        )
        * inv_root
    )
    in_range = (
        blocks[:, None] * PAGE + jnp.arange(PAGE, dtype=jnp.int32)[None, :] < page_length[:, None]
    )
    weights = jnp.where(in_range[:, None, None, :], jnp.exp(scores), 0.0)
    page_total = jnp.sum(weights, axis=-1).reshape(local_pages, H)
    page_weighted = jnp.einsum(
        "skgt,stkd->skgd",
        weights.astype(jnp.bfloat16),
        value_rows,
        preferred_element_type=jnp.float32,
    ).reshape(local_pages, H * HD)
    split_numerator = jnp.einsum(
        "sqp,smc->pmqc",
        chosen_full,
        page_weighted.reshape(local_pages, mp_count, head_cols),
        precision=highest,
    )
    split_numerator = split_numerator.reshape(pool_count * mp_count, group_rows, head_cols)
    split_denominator = jnp.einsum("sqp,sh->pqh", chosen_full, page_total, precision=highest)
    split_denominator = jnp.broadcast_to(
        split_denominator[:, None], (pool_count, mp_count, group_rows, H)
    ).reshape(pool_count * mp_count, group_rows, H)
    denominator_high = split_denominator.astype(jnp.bfloat16)
    denominator_low = (split_denominator - denominator_high.astype(jnp.float32)).astype(
        jnp.bfloat16
    )
    sums = jnp.concatenate(
        [split_numerator.astype(jnp.bfloat16), denominator_high, denominator_low], axis=2
    )
    sums = lax.all_to_all(sums, ("pool", "mp"), 0, 0, tiled=True).astype(jnp.float32)
    sums = jnp.sum(sums, axis=0)
    column_numerator = sums[None, :, :head_cols]
    column_denominator = (
        sums[:, head_cols : head_cols + H] + sums[:, head_cols + H : head_cols + 2 * H]
    )[None]
    own_columns = lax.dynamic_slice_in_dim(own_numerator, mp_index * head_cols, head_cols, 1)
    denominator_cols = lax.dynamic_slice_in_dim(
        jnp.repeat(column_denominator[0] + own_weight, HD, axis=1),
        mp_index * head_cols,
        head_cols,
        1,
    )
    attended = ((column_numerator[0] + own_columns) / denominator_cols).astype(jnp.bfloat16)
    projected = jnp.dot(attended, out_weight, preferred_element_type=jnp.float32)
    sent = projected.astype(jnp.bfloat16)
    summed = projected
    for step in range(1, mp_count):
        ring = [(i, (i + step) % mp_count) for i in range(mp_count)]
        summed = summed + lax.ppermute(sent, "mp", ring).astype(jnp.float32)
    mixed_rows = (wide_rows + summed).astype(jnp.bfloat16)
    normed_two = rms_scale(mixed_rows.astype(jnp.float32), feed_gain, EPS_WIDE).astype(jnp.bfloat16)
    gate_values = jnp.dot(normed_two, gate_weight, preferred_element_type=jnp.float32)
    up_values = jnp.dot(normed_two, up_weight, preferred_element_type=jnp.float32)
    hidden = (jax.nn.silu(gate_values) * up_values).astype(jnp.bfloat16)
    feed_part = jnp.dot(hidden, down_weight, preferred_element_type=jnp.float32)
    feed_sent = feed_part.astype(jnp.bfloat16)
    feed_row = lax.dynamic_slice_in_dim(feed_part, mp_index, 1, 0)
    for step in range(1, mp_count):
        ring = [(i, (i + step) % mp_count) for i in range(mp_count)]
        row = lax.dynamic_slice_in_dim(feed_sent, (mp_index + step) % mp_count, 1, 0)
        feed_row = feed_row + lax.ppermute(row, "mp", ring).astype(jnp.float32)
    own_mixed = lax.dynamic_slice_in_dim(mixed_rows, mp_index, 1, 0)
    hidden_out = (own_mixed.astype(jnp.float32) + feed_row).astype(jnp.bfloat16)
    own_key = lax.dynamic_slice_in_dim(key_new.reshape(group_rows, KVH * HD), mp_index, 1, 0)
    own_value = lax.dynamic_slice_in_dim(value_new.reshape(group_rows, KVH * HD), mp_index, 1, 0)
    new_entries = jnp.concatenate([own_key, own_value], axis=1)
    return (hidden_out, new_entries)


def solution(mesh):
    in_specs = (
        P("pool", None),
        P(),
        P(None, "mp"),
        P(),
        P(),
        P(("pool", "mp"), None, None),
        P(),
        P(),
        P(),
        P("mp", None),
        P(),
        P(None, "mp"),
        P(None, "mp"),
        P("mp", None),
    )
    out_specs = (P(("pool", "mp"), None), P(("pool", "mp"), None))
    return jax.shard_map(shards, mesh=mesh, in_specs=in_specs, out_specs=out_specs, check_vma=False)
```

```python
import jax
import jax.numpy as jnp
import numpy as np
from jax import lax
from jax.experimental import pallas as pl
from jax.experimental.pallas import tpu as pltpu
from jax.sharding import PartitionSpec as P

H = 20
KVH = 5
HD = 64
GROUPS = H // KVH
PAGE = 128
LANES = 128
KEYS = KVH * HD
ENTRY = 2 * KEYS
EPS_WIDE = 1e-05
EPS_HEAD = 1e-06
MIB = 1 << 20

BF16 = jnp.bfloat16
F32 = jnp.float32
I32 = jnp.int32


def up_to(value, step):
    return (value + step - 1) // step * step


def dot(left, right):
    return jnp.dot(left, right, preferred_element_type=F32)


def dot_rows(left, right):
    return lax.dot_general(left, right, (((1,), (1,)), ((), ())), preferred_element_type=F32)


def two_halves(values):
    high = values.astype(BF16)
    return high, (values - high.astype(F32)).astype(BF16)


def lane_iota(shape):
    return lax.broadcasted_iota(I32, shape, len(shape) - 1)


def sublane_iota(shape):
    return lax.broadcasted_iota(I32, shape, len(shape) - 2)


def move_lanes(tile, shift):
    shift %= LANES
    return tile if shift == 0 else pltpu.roll(tile, shift, 1)


def lane_tile(tiles, start, source, step=16):
    spans = []
    for lane in range(0, LANES, step):
        found = source(start + lane)
        piece = None if found is None else (found[0], (lane - found[1]) % LANES)
        if spans and spans[-1][0] == piece:
            spans[-1][2] = lane + step
        else:
            spans.append([piece, lane, lane + step])
    ranges = {}
    for piece, low, high in spans:
        ranges.setdefault(piece, []).append((low, high))
    values = {
        piece: None if piece is None else move_lanes(tiles(piece[0]), piece[1]) for piece in ranges
    }
    like = next(value for value in values.values() if value is not None)
    result = None
    for piece, value in values.items():
        value = jnp.zeros_like(like) if value is None else value
        if result is None:
            result = value
            continue
        lanes = lane_iota(like.shape)
        inside = None
        for low, high in ranges[piece]:
            here = (lanes >= low) & (lanes < high)
            inside = here if inside is None else inside | here
        result = jnp.where(inside, value, result)
    return result


def swap_halves(tile):
    lanes = lane_iota(tile.shape) % HD
    return jnp.where(
        lanes < HD // 2, move_lanes(tile, LANES - HD // 2), move_lanes(tile, HD // 2)
    )


def rms_scale(values, scaling, epsilon):
    mean_square = jnp.mean(values * values, axis=-1, keepdims=True)
    return values * lax.rsqrt(mean_square + epsilon) * scaling


def project_kernel(rows_ref, gain_ref, weight_ref, out_ref):
    normed = rms_scale(rows_ref[...].astype(F32), gain_ref[...], EPS_WIDE).astype(BF16)
    packed = dot_rows(normed, weight_ref[...])
    count, columns = packed.shape
    if count < 8:
        packed = jnp.concatenate([packed] * (8 // count), axis=0)
    out_ref[:, :, :columns] = jnp.broadcast_to(
        packed[None], (out_ref.shape[0],) + packed.shape
    ).astype(BF16)
    rest = out_ref.shape[2] - columns
    if rest:
        out_ref[:, :, columns:] = jnp.zeros((out_ref.shape[0], 8, rest), BF16)


def lookup_kernel(
    place_ref,
    table_ref,
    length_ref,
    order_ref,
    frequency_ref,
    query_gain_ref,
    key_gain_ref,
    query_cos_ref,
    query_sin_ref,
    key_cos_ref,
    key_sin_ref,
    row_ref,
    valid_ref,
    *,
    pages,
):
    slots = row_ref.shape[0]
    requests, blocks = table_ref.shape
    table = table_ref[...]
    first_page, own_row = place_ref[0], place_ref[1]
    entry = (sublane_iota(table.shape) * blocks + lane_iota(table.shape) + 1).astype(F32)
    found = [
        jnp.sum(jnp.where(table == first_page + slot, entry, 0.0), axis=0, keepdims=True)
        for slot in range(pages)
    ]
    found.append(jnp.zeros((slots - pages, blocks), F32))
    found = jnp.sum(jnp.concatenate(found, axis=0), axis=1, keepdims=True).astype(I32) - 1
    slot = sublane_iota((slots, 1))
    order = order_ref[...]
    lanes = lane_iota(order.shape)
    own_request = jnp.sum(
        jnp.where(lanes == own_row, order, 0).astype(F32), axis=1, keepdims=True
    ).astype(I32)
    request = jnp.where(slot == pages, own_request, jnp.where(found < 0, -1, found // blocks))
    block = jnp.where(found < 0, 0, found % blocks)
    lane_full = lane_iota((slots, requests))
    length = jnp.sum(
        jnp.where(lane_full == request, length_ref[...].astype(F32), 0.0), axis=1, keepdims=True
    )
    row = jnp.sum(
        jnp.where(order == request, lane_full.astype(F32), 0.0), axis=1, keepdims=True
    ).astype(I32)
    row = jnp.where(request < 0, -1, row)
    valid = jnp.clip(length.astype(I32) - block * PAGE, 0, PAGE)
    valid = jnp.where(slot == pages, 1, jnp.where(request < 0, 0, valid))
    angles = length * frequency_ref[...]
    cosines, sines = jnp.cos(angles), jnp.sin(angles)
    half = lane_iota(angles.shape) % HD
    sines = jnp.where(half < HD // 2, -sines, sines)
    for gain_ref, cos_ref, sin_ref, factor in (
        (query_gain_ref, query_cos_ref, query_sin_ref, HD ** (-0.5)),
        (key_gain_ref, key_cos_ref, key_sin_ref, 1.0),
    ):
        gain = jnp.broadcast_to(gain_ref[...] * factor, (8, HD))
        gain = jnp.concatenate([gain, gain], axis=1)
        cos_ref[...] = cosines * gain[:1]
        sin_ref[...] = sines * swap_halves(gain)[:1]
    row_ref[...] = jnp.broadcast_to(row, row_ref.shape)
    valid_ref[...] = jnp.broadcast_to(valid, valid_ref.shape)


def attend_kernel(
    packed_ref,
    page_ref,
    query_cos_ref,
    query_sin_ref,
    key_cos_ref,
    key_sin_ref,
    row_ref,
    valid_ref,
    sums_ref,
    entry_ref,
    query_ref,
    fresh_ref,
    partial_ref,
    *,
    pool_count,
    mp_count,
    group_rows,
    columns,
):
    pages = page_ref.shape[0]
    slots = row_ref.shape[0]
    row = row_ref[...][:, :1]
    total_rows = packed_ref.shape[0]
    source = lane_iota((slots, total_rows))
    source_row = source // (mp_count * group_rows) * group_rows + source % group_rows
    source_part = source // group_rows % mp_count
    hit = source_row == row
    choose = jnp.concatenate(
        [jnp.where(hit & (source_part == part), 1.0, 0.0) for part in range(mp_count)], axis=0
    ).astype(BF16)
    chosen = dot(choose, packed_ref[...])

    def part_tile(key):
        part, tile = key
        return chosen[part * slots : (part + 1) * slots, tile * LANES : (tile + 1) * LANES]

    def part_source(column):
        part, local = divmod(column, columns)
        return (part, local // LANES), local % LANES

    tile_count = (H * HD + ENTRY) // LANES
    query_tiles = H * HD // LANES
    key_tiles = up_to(KEYS, LANES) // LANES
    tiles = [lane_tile(part_tile, t * LANES, part_source) for t in range(tile_count)]
    stacked = jnp.concatenate(tiles[: query_tiles + key_tiles], axis=0)
    ones = jnp.where(
        sublane_iota((LANES, LANES)) // HD == lane_iota((LANES, LANES)) // HD, 1.0, 0.0
    ).astype(BF16)
    high, low = two_halves(stacked * stacked)
    scale = lax.rsqrt((dot(high, ones) + dot(low, ones)) * (1.0 / HD) + EPS_HEAD)
    swapped = swap_halves(stacked)
    split = query_tiles * slots

    def turned(low, high, cos_ref, sin_ref):
        shape = ((high - low) // slots, slots, LANES)
        value = stacked[low:high].reshape(shape) * cos_ref[...][None]
        value = value + swapped[low:high].reshape(shape) * sin_ref[...][None]
        return (value * scale[low:high].reshape(shape)).astype(BF16).astype(F32)

    queries = turned(0, split, query_cos_ref, query_sin_ref)
    keys = turned(split, stacked.shape[0], key_cos_ref, key_sin_ref)
    middle = jnp.where(lane_iota((slots, LANES)) < KEYS % LANES, keys[-1], tiles[-key_tiles])
    entries = [keys[t] for t in range(key_tiles - 1)] + [middle] + tiles[-(key_tiles - 1) :]
    fresh = jnp.concatenate(entries, axis=1)[pages : pages + 8]
    entry_ref[...] = fresh[:1].astype(BF16)
    fresh = jnp.where(sublane_iota(fresh.shape) == 0, fresh, 0.0)
    fresh_ref[...] = jnp.concatenate([fresh, jnp.zeros_like(fresh)], axis=0).astype(BF16)

    wide = key_tiles * LANES
    for member in range(GROUPS):

        def query_source(column):
            kv = column // HD
            if kv >= KVH:
                return None
            head = kv * GROUPS + member
            return head // 2, head % 2 * HD + column % HD

        query_ref[member] = jnp.concatenate(
            [
                lane_tile(lambda t: queries[t], t * LANES, query_source)
                for t in range(key_tiles)
            ],
            axis=1,
        )

    key_mask = lane_iota((8, wide)) // HD == sublane_iota((8, wide))
    value_skip = wide - KEYS
    value_mask = (lane_iota((8, wide)) + (HD - value_skip)) // HD == sublane_iota((8, wide)) + 1
    total_mask = (lane_iota((8, wide)) == sublane_iota((8, wide))) & (
        sublane_iota((8, wide)) < KVH
    )
    value_mask = value_mask & (sublane_iota((8, wide)) < KVH)
    for slot in range(pages + 1):
        spread = jnp.concatenate(
            [
                jnp.where(
                    key_mask,
                    jnp.broadcast_to(query_ref[member, slot : slot + 1, :], (8, wide)),
                    0.0,
                )
                for member in range(GROUPS)
            ],
            axis=0,
        ).astype(BF16)
        if slot < pages:
            key_rows = page_ref[slot, :, :wide]
            value_rows = page_ref[slot, :, ENTRY - wide :]
        else:
            key_rows = fresh_ref[:, :wide]
            value_rows = fresh_ref[:, ENTRY - wide :]
        scores = dot_rows(spread, key_rows)
        count = valid_ref[slot : slot + 1, : scores.shape[1]]
        weights = jnp.where(lane_iota(scores.shape) < count, jnp.exp(scores), 0.0)
        totals = jnp.sum(weights, axis=1, keepdims=True)
        weighted = dot(weights.astype(BF16), value_rows)
        for member in range(GROUPS):
            low = member * 8
            kept = jnp.where(value_mask, weighted[low : low + 8], 0.0)
            kept = jnp.where(total_mask, totals[low : low + 8], kept)
            partial_ref[member, slot * 8 : slot * 8 + 8, :] = kept

    depth = partial_ref.shape[1]
    spread_row = jnp.sum(
        jnp.where(
            lane_iota((slots, depth)) // 8 == sublane_iota((slots, depth)),
            jnp.broadcast_to(row, (slots, depth)).astype(F32),
            0.0,
        ),
        axis=0,
        keepdims=True,
    ).astype(I32)
    copies = 8 // group_rows
    place = sublane_iota((pool_count * 8, depth))
    place = place // 8 * group_rows + place % group_rows
    collect = jnp.where(place == spread_row, 1.0, 0.0).astype(BF16)
    summed = []
    for member in range(GROUPS):
        high, low = two_halves(partial_ref[member])
        summed.append(dot(collect, high) + dot(collect, low))
    first = lane_iota((pool_count * 8, LANES)) < KVH
    totals = None
    for member in range(GROUPS):
        moved = move_lanes(jnp.where(first, summed[member][:, :LANES], 0.0), KVH * member)
        totals = moved if totals is None else totals + moved
    rounded = totals.astype(BF16).astype(F32)
    totals = rounded + move_lanes(totals - rounded, H)

    head_cols = H * HD // mp_count
    width = sums_ref.shape[3]

    def sum_tile(key):
        if key == "totals":
            return totals
        member, tile = key
        return summed[member][:, tile * LANES : (tile + 1) * LANES]

    for pair in range(mp_count // copies):
        parts = []
        for part in range(pair * copies, (pair + 1) * copies):

            def sum_source(column):
                if column >= head_cols:
                    lane = column - head_cols
                    return ("totals", lane) if lane < 2 * H else None
                kv, member = divmod((part * head_cols + column) // HD, GROUPS)
                lane = value_skip + kv * HD + (part * head_cols + column) % HD
                return (member, lane // LANES), lane % LANES

            parts.append(
                jnp.concatenate(
                    [lane_tile(sum_tile, start, sum_source) for start in range(0, width, LANES)],
                    axis=1,
                )
            )
        block = parts[0]
        for index in range(1, copies):
            block = jnp.where(
                sublane_iota(block.shape) % 8 >= index * group_rows, parts[index], block
            )
        sums_ref[:, pair] = block.reshape(pool_count, 8, width).astype(BF16)


def mix_kernel(place_ref, sums_ref, hidden_ref, weight_ref, kept_ref, sent_ref):
    total_rows, width = sums_ref.shape
    head_cols = weight_ref.shape[0]
    group_rows = hidden_ref.shape[0]
    part = place_ref[2]
    same = jnp.where(
        lane_iota((8, total_rows)) % group_rows == sublane_iota((8, total_rows)) % group_rows,
        1.0,
        0.0,
    ).astype(BF16)
    sums = dot(same, sums_ref[...])
    tile = head_cols // LANES * LANES
    totals = sums[:, tile : tile + LANES]
    column = lane_iota((LANES, head_cols)) + part * head_cols
    head = column // HD
    lane = sublane_iota((LANES, head_cols)) - (head_cols - tile)
    index = head % GROUPS * KVH + head // GROUPS
    spread = jnp.where((lane == index) | (lane == index + H), 1.0, 0.0).astype(BF16)
    high = totals.astype(BF16)
    middle, low = two_halves(totals - high.astype(F32))
    denominator = dot(high, spread) + dot(middle, spread) + dot(low, spread)
    attended = (sums[:, :head_cols] / denominator).astype(BF16)
    projected = dot(attended, weight_ref[...])[:group_rows]
    kept_ref[...] = projected + hidden_ref[...].astype(F32)
    sent_ref[...] = projected.astype(BF16)


def feed_kernel(place_ref, *refs, steps):
    kept_ref, *arrived = refs[: steps + 1]
    gain_ref, gate_ref, up_ref, down_ref = refs[steps + 1 : steps + 5]
    base_ref, *sent = refs[steps + 5 : 2 * steps + 6]
    part_ref = refs[-1]
    group_rows = kept_ref.shape[0]
    part = place_ref[2]
    mixed = kept_ref[...]
    for ref in arrived:
        mixed = mixed + ref[...].astype(F32)
    mixed = mixed.astype(BF16).astype(F32)
    normed = rms_scale(mixed, gain_ref[...], EPS_WIDE).astype(BF16)
    gate = dot(normed, gate_ref[...])
    up = dot(normed, up_ref[...])
    hidden = (gate * jax.nn.sigmoid(gate) * up).astype(BF16)
    part_ref[:group_rows] = dot(hidden, down_ref[...])
    own = part_ref[pl.ds(part, 1), :]
    for step, ref in enumerate(sent):
        target = lax.rem(part + (step + 1), steps + 1)
        ref[...] = part_ref[pl.ds(target, 1), :].astype(BF16)
    part_ref[:group_rows] = mixed
    base_ref[...] = own + part_ref[pl.ds(part, 1), :]


def in_vmem(count):
    return [pl.BlockSpec(memory_space=pltpu.VMEM)] * count


SCALARS = pl.BlockSpec(memory_space=pltpu.SMEM)


def params(limit):
    return pltpu.CompilerParams(vmem_limit_bytes=limit * MIB)


def shards(
    hidden_in,
    mix_gain,
    project_in,
    query_gain,
    key_gain,
    page_cache,
    page_table,
    lengths,
    row_order,
    out_weight,
    feed_gain,
    gate_weight,
    up_weight,
    down_weight,
):
    pool_count = lax.axis_size("pool")
    mp_count = lax.axis_size("mp")
    devices = pool_count * mp_count
    device = lax.axis_index("pool") * mp_count + lax.axis_index("mp")
    group_rows, model = hidden_in.shape
    pages = page_cache.shape[0]
    requests = lengths.shape[0]
    columns = project_in.shape[1]
    padded = up_to(columns, LANES)
    head_cols = H * HD // mp_count
    width = up_to(head_cols + 2 * H, LANES)
    slots = up_to(pages + 1, 8)
    total_rows = devices * group_rows
    everyone = ("pool", "mp")
    place = jnp.stack([device * pages, device, lax.axis_index("mp")]).astype(I32)
    exponent = np.arange(LANES) % (HD // 2) * (-2.0 / HD)
    frequency = jnp.asarray((10000.0**exponent).astype(np.float32)[None])

    packed = pl.pallas_call(
        project_kernel,
        out_shape=jax.ShapeDtypeStruct((total_rows // 8, 8, padded), BF16),
        in_specs=in_vmem(3),
        out_specs=in_vmem(1)[0],
        compiler_params=params(8),
        name="project",
    )(hidden_in, mix_gain[None], project_in.T)
    packed = lax.all_to_all(
        packed.reshape(devices, group_rows, padded), everyone, 0, 0, tiled=True
    )

    table = jax.ShapeDtypeStruct((slots, LANES), F32)
    index = jax.ShapeDtypeStruct((slots, LANES), I32)
    found = pl.pallas_call(
        lambda *refs: lookup_kernel(*refs, pages=pages),
        out_shape=(table, table, table, table, index, index),
        in_specs=[SCALARS] + in_vmem(6),
        out_specs=in_vmem(6),
        compiler_params=params(4),
        cost_estimate=pl.CostEstimate(flops=10_000_000, bytes_accessed=10_000_000, transcendentals=0),
        name="lookup",
    )(
        place,
        page_table,
        lengths[None],
        row_order[None],
        frequency,
        query_gain[None],
        key_gain[None],
    )

    copies = 8 // group_rows
    wide = up_to(KEYS, LANES)
    sums, new_entries = pl.pallas_call(
        lambda *refs: attend_kernel(
            *refs,
            pool_count=pool_count,
            mp_count=mp_count,
            group_rows=group_rows,
            columns=columns,
        ),
        out_shape=(
            jax.ShapeDtypeStruct((pool_count, mp_count // copies, 8, width), BF16),
            jax.ShapeDtypeStruct((1, ENTRY), BF16),
        ),
        in_specs=in_vmem(8),
        out_specs=in_vmem(2),
        scratch_shapes=[
            pltpu.VMEM((GROUPS, slots, wide), F32),
            pltpu.VMEM((16, ENTRY), BF16),
            pltpu.VMEM((GROUPS, (pages + 1) * 8, wide), F32),
        ],
        compiler_params=params(16),
        name="attend",
    )(packed.reshape(total_rows, padded), page_cache, *found)
    sums = lax.all_to_all(
        sums.reshape(devices, group_rows, width), everyone, 0, 0, tiled=True
    )

    kept, sent = pl.pallas_call(
        mix_kernel,
        out_shape=(
            jax.ShapeDtypeStruct((group_rows, model), F32),
            jax.ShapeDtypeStruct((group_rows, model), BF16),
        ),
        in_specs=[SCALARS] + in_vmem(3),
        out_specs=in_vmem(2),
        compiler_params=params(8),
        name="mix",
    )(place, sums.reshape(total_rows, width), hidden_in, out_weight)

    def ring(value, step):
        return lax.ppermute(value, "mp", [(i, (i + step) % mp_count) for i in range(mp_count)])

    steps = mp_count - 1
    arrived = [ring(sent, step) for step in range(1, mp_count)]
    base, *rows = pl.pallas_call(
        lambda *refs: feed_kernel(*refs, steps=steps),
        out_shape=(jax.ShapeDtypeStruct((1, model), F32),)
        + (jax.ShapeDtypeStruct((1, model), BF16),) * steps,
        in_specs=[SCALARS] + in_vmem(steps + 5),
        out_specs=in_vmem(steps + 1),
        scratch_shapes=[pltpu.VMEM((8, model), F32)],
        compiler_params=params(24),
        name="feed",
    )(place, kept, *arrived, feed_gain[None], gate_weight, up_weight, down_weight)
    for step, row in enumerate(rows):
        base = base + ring(row, step + 1).astype(F32)
    return (base.astype(BF16), new_entries)


def solution(mesh):
    in_specs = (
        P("pool", None),
        P(),
        P(None, "mp"),
        P(),
        P(),
        P(("pool", "mp"), None, None),
        P(),
        P(),
        P(),
        P("mp", None),
        P(),
        P(None, "mp"),
        P(None, "mp"),
        P("mp", None),
    )
    out_specs = (P(("pool", "mp"), None), P(("pool", "mp"), None))
    return jax.shard_map(shards, mesh=mesh, in_specs=in_specs, out_specs=out_specs, check_vma=False)
```

```python
import jax
import jax.numpy as jnp
import numpy as np
from jax import lax
from jax.experimental import pallas as pl
from jax.experimental.pallas import tpu as pltpu
from jax.sharding import PartitionSpec as P

H = 20
KVH = 5
HD = 64
GROUPS = H // KVH
PAGE = 128
LANES = 128
KEYS = KVH * HD
ENTRY = 2 * KEYS
EPS_WIDE = 1e-05
EPS_HEAD = 1e-06
MIB = 1 << 20

BF16 = jnp.bfloat16
F32 = jnp.float32
I32 = jnp.int32


def up_to(value, step):
    return (value + step - 1) // step * step


def dot(left, right):
    return jnp.dot(left, right, preferred_element_type=F32)


def dot_rows(left, right):
    return lax.dot_general(left, right, (((1,), (1,)), ((), ())), preferred_element_type=F32)


def two_halves(values):
    high = values.astype(BF16)
    return high, (values - high.astype(F32)).astype(BF16)


def lane_iota(shape):
    return lax.broadcasted_iota(I32, shape, len(shape) - 1)


def sublane_iota(shape):
    return lax.broadcasted_iota(I32, shape, len(shape) - 2)


def move_lanes(tile, shift):
    shift %= LANES
    return tile if shift == 0 else pltpu.roll(tile, shift, 1)


def lane_tile(tiles, start, source, step=16):
    spans = []
    for lane in range(0, LANES, step):
        found = source(start + lane)
        piece = None if found is None else (found[0], (lane - found[1]) % LANES)
        if spans and spans[-1][0] == piece:
            spans[-1][2] = lane + step
        else:
            spans.append([piece, lane, lane + step])
    ranges = {}
    for piece, low, high in spans:
        ranges.setdefault(piece, []).append((low, high))
    values = {
        piece: None if piece is None else move_lanes(tiles(piece[0]), piece[1]) for piece in ranges
    }
    like = next(value for value in values.values() if value is not None)
    result = None
    for piece, value in values.items():
        value = jnp.zeros_like(like) if value is None else value
        if result is None:
            result = value
            continue
        lanes = lane_iota(like.shape)
        inside = None
        for low, high in ranges[piece]:
            here = (lanes >= low) & (lanes < high)
            inside = here if inside is None else inside | here
        result = jnp.where(inside, value, result)
    return result


def swap_halves(tile):
    lanes = lane_iota(tile.shape) % HD
    return jnp.where(
        lanes < HD // 2, move_lanes(tile, LANES - HD // 2), move_lanes(tile, HD // 2)
    )


def rms_scale(values, scaling, epsilon):
    mean_square = jnp.mean(values * values, axis=-1, keepdims=True)
    return values * lax.rsqrt(mean_square + epsilon) * scaling


def copy_in(source, target, semaphore):
    copy = pltpu.make_async_copy(source, target, semaphore)
    copy.start()
    return copy


def project_kernel(
    rows_hbm, gain_hbm, weight_hbm, out_ref, rows_ref, gain_ref, weight_ref, semaphores
):
    columns = weight_ref.shape[0]
    chunk = up_to(columns // 4, 16)
    first = [
        copy_in(rows_hbm, rows_ref, semaphores.at[0]),
        copy_in(gain_hbm, gain_ref, semaphores.at[1]),
    ]
    starts = range(0, columns, chunk)
    copies = []
    for index, start in enumerate(starts):
        part = pl.ds(start, min(chunk, columns - start))
        copies.append(
            copy_in(weight_hbm.at[part], weight_ref.at[part], semaphores.at[2 + index])
        )
    for copy in first:
        copy.wait()
    normed = rms_scale(rows_ref[...].astype(F32), gain_ref[...], EPS_WIDE).astype(BF16)
    devices, count, padded = out_ref.shape
    if padded > columns:
        out_ref[:, :, columns:] = jnp.zeros((devices, count, padded - columns), BF16)
    for copy, start in zip(copies, starts):
        copy.wait()
        stop = min(start + chunk, columns)
        packed = dot_rows(normed, weight_ref[start:stop])
        out_ref[:, :, start:stop] = jnp.broadcast_to(
            packed.astype(BF16)[None], (devices, count, stop - start)
        )


def lookup_kernel(*refs, pages):
    sources, outputs, scratch = refs[:7], refs[7:14], refs[14:]
    (
        query_cos_ref,
        query_sin_ref,
        key_cos_ref,
        key_sin_ref,
        row_ref,
        valid_ref,
        page_ref,
    ) = outputs
    table_ref, length_ref, order_ref, frequency_ref, query_gain_ref, key_gain_ref = scratch[:6]
    semaphores = scratch[6]
    small = [
        copy_in(source, target, semaphores.at[index])
        for index, (source, target) in enumerate(zip(sources[:6], scratch[:6]))
    ]
    step = up_to(pages, 4) // 4
    large = [
        copy_in(
            sources[6].at[pl.ds(start, step)],
            page_ref.at[pl.ds(start, step)],
            semaphores.at[6 + start // step],
        )
        for start in range(0, pages, step)
    ]
    for copy in small:
        copy.wait()
    device = lax.axis_index("pool") * lax.axis_size("mp") + lax.axis_index("mp")
    slots = row_ref.shape[0]
    requests, blocks = table_ref.shape
    table = table_ref[...]
    first_page, own_row = device * pages, device
    entry = (sublane_iota(table.shape) * blocks + lane_iota(table.shape) + 1).astype(F32)
    found = [
        jnp.sum(jnp.where(table == first_page + slot, entry, 0.0), axis=0, keepdims=True)
        for slot in range(pages)
    ]
    found.append(jnp.zeros((slots - pages, blocks), F32))
    found = jnp.sum(jnp.concatenate(found, axis=0), axis=1, keepdims=True).astype(I32) - 1
    slot = sublane_iota((slots, 1))
    order = order_ref[...]
    lanes = lane_iota(order.shape)
    own_request = jnp.sum(
        jnp.where(lanes == own_row, order, 0).astype(F32), axis=1, keepdims=True
    ).astype(I32)
    request = jnp.where(slot == pages, own_request, jnp.where(found < 0, -1, found // blocks))
    block = jnp.where(found < 0, 0, found % blocks)
    lane_full = lane_iota((slots, requests))
    length = jnp.sum(
        jnp.where(lane_full == request, length_ref[...].astype(F32), 0.0), axis=1, keepdims=True
    )
    row = jnp.sum(
        jnp.where(order == request, lane_full.astype(F32), 0.0), axis=1, keepdims=True
    ).astype(I32)
    row = jnp.where(request < 0, -1, row)
    valid = jnp.clip(length.astype(I32) - block * PAGE, 0, PAGE)
    valid = jnp.where(slot == pages, 1, jnp.where(request < 0, 0, valid))
    angles = length * frequency_ref[...]
    cosines, sines = jnp.cos(angles), jnp.sin(angles)
    half = lane_iota(angles.shape) % HD
    sines = jnp.where(half < HD // 2, -sines, sines)
    for gain_ref, cos_ref, sin_ref, factor in (
        (query_gain_ref, query_cos_ref, query_sin_ref, HD ** (-0.5)),
        (key_gain_ref, key_cos_ref, key_sin_ref, 1.0),
    ):
        gain = jnp.broadcast_to(gain_ref[...] * factor, (8, HD))
        gain = jnp.concatenate([gain, gain], axis=1)
        cos_ref[...] = cosines * gain[:1]
        sin_ref[...] = sines * swap_halves(gain)[:1]
    row_ref[...] = jnp.broadcast_to(row, row_ref.shape)
    valid_ref[...] = jnp.broadcast_to(valid, valid_ref.shape)
    for copy in large:
        copy.wait()


def attend_kernel(
    packed_ref,
    page_ref,
    query_cos_ref,
    query_sin_ref,
    key_cos_ref,
    key_sin_ref,
    row_ref,
    valid_ref,
    sums_ref,
    entry_ref,
    query_ref,
    fresh_ref,
    partial_ref,
    *,
    pool_count,
    mp_count,
    group_rows,
    columns,
):
    pages = page_ref.shape[0]
    slots = row_ref.shape[0]
    row = row_ref[...][:, :1]
    total_rows = packed_ref.shape[0] * packed_ref.shape[1]
    packed = packed_ref[...].reshape(total_rows, packed_ref.shape[2])
    source = lane_iota((slots, total_rows))
    source_row = source // (mp_count * group_rows) * group_rows + source % group_rows
    source_part = source // group_rows % mp_count
    hit = source_row == row
    choose = jnp.concatenate(
        [jnp.where(hit & (source_part == part), 1.0, 0.0) for part in range(mp_count)], axis=0
    ).astype(BF16)
    chosen = dot(choose, packed)

    def part_tile(key):
        part, tile = key
        return chosen[part * slots : (part + 1) * slots, tile * LANES : (tile + 1) * LANES]

    def part_source(column):
        part, local = divmod(column, columns)
        return (part, local // LANES), local % LANES

    tile_count = (H * HD + ENTRY) // LANES
    query_tiles = H * HD // LANES
    key_tiles = up_to(KEYS, LANES) // LANES
    tiles = [lane_tile(part_tile, t * LANES, part_source) for t in range(tile_count)]
    stacked = jnp.concatenate(tiles[: query_tiles + key_tiles], axis=0)
    ones = jnp.where(
        sublane_iota((LANES, LANES)) // HD == lane_iota((LANES, LANES)) // HD, 1.0, 0.0
    ).astype(BF16)
    high, low = two_halves(stacked * stacked)
    scale = lax.rsqrt((dot(high, ones) + dot(low, ones)) * (1.0 / HD) + EPS_HEAD)
    swapped = swap_halves(stacked)
    split = query_tiles * slots

    def turned(low, high, cos_ref, sin_ref):
        shape = ((high - low) // slots, slots, LANES)
        value = stacked[low:high].reshape(shape) * cos_ref[...][None]
        value = value + swapped[low:high].reshape(shape) * sin_ref[...][None]
        return (value * scale[low:high].reshape(shape)).astype(BF16).astype(F32)

    queries = turned(0, split, query_cos_ref, query_sin_ref)
    keys = turned(split, stacked.shape[0], key_cos_ref, key_sin_ref)
    middle = jnp.where(lane_iota((slots, LANES)) < KEYS % LANES, keys[-1], tiles[-key_tiles])
    entries = [keys[t] for t in range(key_tiles - 1)] + [middle] + tiles[-(key_tiles - 1) :]
    fresh = jnp.concatenate(entries, axis=1)[pages : pages + 8]
    entry_ref[...] = fresh[:1].astype(BF16)
    fresh = jnp.where(sublane_iota(fresh.shape) == 0, fresh, 0.0)
    fresh_ref[...] = jnp.concatenate([fresh, jnp.zeros_like(fresh)], axis=0).astype(BF16)

    wide = key_tiles * LANES
    for member in range(GROUPS):

        def query_source(column):
            kv = column // HD
            if kv >= KVH:
                return None
            head = kv * GROUPS + member
            return head // 2, head % 2 * HD + column % HD

        query_ref[member] = jnp.concatenate(
            [
                lane_tile(lambda t: queries[t], t * LANES, query_source)
                for t in range(key_tiles)
            ],
            axis=1,
        )

    key_mask = lane_iota((8, wide)) // HD == sublane_iota((8, wide))
    value_skip = wide - KEYS
    value_mask = (lane_iota((8, wide)) + (HD - value_skip)) // HD == sublane_iota((8, wide)) + 1
    total_mask = (lane_iota((8, wide)) == sublane_iota((8, wide))) & (
        sublane_iota((8, wide)) < KVH
    )
    value_mask = value_mask & (sublane_iota((8, wide)) < KVH)
    for slot in range(pages + 1):
        spread = jnp.concatenate(
            [
                jnp.where(
                    key_mask,
                    jnp.broadcast_to(query_ref[member, slot : slot + 1, :], (8, wide)),
                    0.0,
                )
                for member in range(GROUPS)
            ],
            axis=0,
        ).astype(BF16)
        if slot < pages:
            key_rows = page_ref[slot, :, :wide]
            value_rows = page_ref[slot, :, ENTRY - wide :]
        else:
            key_rows = fresh_ref[:, :wide]
            value_rows = fresh_ref[:, ENTRY - wide :]
        scores = dot_rows(spread, key_rows)
        count = valid_ref[slot : slot + 1, : scores.shape[1]]
        weights = jnp.where(lane_iota(scores.shape) < count, jnp.exp(scores), 0.0)
        totals = jnp.sum(weights, axis=1, keepdims=True)
        weighted = dot(weights.astype(BF16), value_rows)
        for member in range(GROUPS):
            low = member * 8
            kept = jnp.where(value_mask, weighted[low : low + 8], 0.0)
            kept = jnp.where(total_mask, totals[low : low + 8], kept)
            partial_ref[member, slot * 8 : slot * 8 + 8, :] = kept

    depth = partial_ref.shape[1]
    spread_row = jnp.sum(
        jnp.where(
            lane_iota((slots, depth)) // 8 == sublane_iota((slots, depth)),
            jnp.broadcast_to(row, (slots, depth)).astype(F32),
            0.0,
        ),
        axis=0,
        keepdims=True,
    ).astype(I32)
    place = sublane_iota((pool_count * 8, depth))
    place = place // 8 * group_rows + place % group_rows
    collect = jnp.where(place == spread_row, 1.0, 0.0).astype(BF16)
    summed = []
    for member in range(GROUPS):
        high, low = two_halves(partial_ref[member])
        summed.append(dot(collect, high) + dot(collect, low))
    first = lane_iota((pool_count * 8, LANES)) < KVH
    totals = None
    for member in range(GROUPS):
        moved = move_lanes(jnp.where(first, summed[member][:, :LANES], 0.0), KVH * member)
        totals = moved if totals is None else totals + moved
    rounded = totals.astype(BF16).astype(F32)
    totals = rounded + move_lanes(totals - rounded, H)

    head_cols = H * HD // mp_count
    width = sums_ref.shape[3]

    def sum_tile(key):
        if key == "totals":
            return totals
        member, tile = key
        return summed[member][:, tile * LANES : (tile + 1) * LANES]

    for part in range(mp_count):

        def sum_source(column):
            if column >= head_cols:
                lane = column - head_cols
                return ("totals", lane) if lane < 2 * H else None
            kv, member = divmod((part * head_cols + column) // HD, GROUPS)
            lane = value_skip + kv * HD + (part * head_cols + column) % HD
            return (member, lane // LANES), lane % LANES

        block = jnp.concatenate(
            [lane_tile(sum_tile, start, sum_source) for start in range(0, width, LANES)], axis=1
        )
        block = block.reshape(pool_count, 8, width)[:, :group_rows]
        sums_ref[:, part] = block.astype(BF16)


def mix_kernel(sums_ref, hidden_ref, weight_ref, kept_ref, sent_ref):
    head_cols = weight_ref.shape[0]
    group_rows = hidden_ref.shape[0]
    part = lax.axis_index("mp")
    sums = jnp.sum(sums_ref[...].astype(F32), axis=0)
    tile = head_cols // LANES * LANES
    totals = sums[:, tile : tile + LANES]
    column = lane_iota((LANES, head_cols)) + part * head_cols
    head = column // HD
    lane = sublane_iota((LANES, head_cols)) - (head_cols - tile)
    index = head % GROUPS * KVH + head // GROUPS
    spread = jnp.where((lane == index) | (lane == index + H), 1.0, 0.0).astype(BF16)
    high = totals.astype(BF16)
    middle, low = two_halves(totals - high.astype(F32))
    denominator = dot(high, spread) + dot(middle, spread) + dot(low, spread)
    attended = (sums[:, :head_cols] / denominator).astype(BF16)
    projected = dot(attended, weight_ref[...])
    kept_ref[...] = projected + hidden_ref[...].astype(F32)
    sent_ref[...] = projected.astype(BF16)


def feed_kernel(*refs, steps):
    kept_ref, *arrived = refs[: steps + 1]
    gain_ref, gate_ref, up_ref, down_ref = refs[steps + 1 : steps + 5]
    base_ref, *sent = refs[steps + 5 : 2 * steps + 6]
    part_ref = refs[-1]
    group_rows = kept_ref.shape[0]
    part = lax.axis_index("mp")
    mixed = kept_ref[...]
    for ref in arrived:
        mixed = mixed + ref[...].astype(F32)
    mixed = mixed.astype(BF16).astype(F32)
    normed = rms_scale(mixed, gain_ref[...], EPS_WIDE).astype(BF16)
    gate = dot(normed, gate_ref[...])
    up = dot(normed, up_ref[...])
    hidden = (gate * jax.nn.sigmoid(gate) * up).astype(BF16)
    part_ref[:group_rows] = dot(hidden, down_ref[...])
    own = part_ref[pl.ds(part, 1), :]
    for step, ref in enumerate(sent):
        target = lax.rem(part + (step + 1), steps + 1)
        ref[...] = part_ref[pl.ds(target, 1), :].astype(BF16)
    part_ref[:group_rows] = mixed
    base_ref[...] = own + part_ref[pl.ds(part, 1), :]


def in_vmem(count):
    return [pl.BlockSpec(memory_space=pltpu.VMEM)] * count


def in_hbm(count):
    return [pl.BlockSpec(memory_space=pltpu.HBM)] * count


def params(limit):
    return pltpu.CompilerParams(vmem_limit_bytes=limit * MIB)


def cost(count):
    return pl.CostEstimate(flops=count, bytes_accessed=0, transcendentals=0)


def like(array):
    return jax.ShapeDtypeStruct(array.shape, array.dtype)


def far(*arrays):
    return [pltpu.with_memory_space_constraint(array, pltpu.HBM) for array in arrays]


def near(*arrays):
    return [pltpu.with_memory_space_constraint(array, pltpu.VMEM) for array in arrays]


def room(array):
    return pltpu.VMEM(array.shape, array.dtype)


def shards(
    hidden_in,
    mix_gain,
    project_in,
    query_gain,
    key_gain,
    page_cache,
    page_table,
    lengths,
    row_order,
    out_weight,
    feed_gain,
    gate_weight,
    up_weight,
    down_weight,
):
    pool_count = lax.axis_size("pool")
    mp_count = lax.axis_size("mp")
    devices = pool_count * mp_count
    group_rows, model = hidden_in.shape
    pages = page_cache.shape[0]
    columns = project_in.shape[1]
    padded = up_to(columns, LANES)
    head_cols = H * HD // mp_count
    width = up_to(head_cols + 2 * H, LANES)
    slots = up_to(pages + 1, 8)
    everyone = ("pool", "mp")
    exponent = np.arange(LANES) % (HD // 2) * (-2.0 / HD)
    frequency = jnp.asarray((10000.0**exponent).astype(np.float32)[None])

    operands = (hidden_in, mix_gain[None], project_in.T)
    packed = pl.pallas_call(
        project_kernel,
        out_shape=jax.ShapeDtypeStruct((devices, group_rows, padded), BF16),
        in_specs=in_hbm(3),
        out_specs=in_vmem(1)[0],
        scratch_shapes=[room(x) for x in operands] + [pltpu.SemaphoreType.DMA((8,))],
        compiler_params=params(8),
        name="project",
    )(*far(*operands))
    packed = lax.all_to_all(packed, everyone, 0, 0, tiled=True)

    table = jax.ShapeDtypeStruct((slots, LANES), F32)
    index = jax.ShapeDtypeStruct((slots, LANES), I32)
    operands = (
        page_table,
        lengths[None],
        row_order[None],
        frequency,
        query_gain[None],
        key_gain[None],
    )
    *found, cached = pl.pallas_call(
        lambda *refs: lookup_kernel(*refs, pages=pages),
        out_shape=(table, table, table, table, index, index, room(page_cache)),
        in_specs=in_hbm(7),
        out_specs=in_vmem(7),
        scratch_shapes=[room(x) for x in operands] + [pltpu.SemaphoreType.DMA((10,))],
        compiler_params=params(8),
        cost_estimate=cost(10_000_000),
        name="lookup",
    )(*far(*operands, page_cache))

    wide = up_to(KEYS, LANES)
    sums, new_entries = pl.pallas_call(
        lambda *refs: attend_kernel(
            *refs,
            pool_count=pool_count,
            mp_count=mp_count,
            group_rows=group_rows,
            columns=columns,
        ),
        out_shape=(
            jax.ShapeDtypeStruct((pool_count, mp_count, group_rows, width), BF16),
            jax.ShapeDtypeStruct((1, ENTRY), BF16),
        ),
        in_specs=in_vmem(8),
        out_specs=in_vmem(2),
        scratch_shapes=[
            pltpu.VMEM((GROUPS, slots, wide), F32),
            pltpu.VMEM((16, ENTRY), BF16),
            pltpu.VMEM((GROUPS, (pages + 1) * 8, wide), F32),
        ],
        compiler_params=params(16),
        cost_estimate=cost(20_000_000_000),
        name="attend",
    )(
        packed,
        *near(cached),
        *found,
    )
    sums = lax.all_to_all(
        sums.reshape(devices, group_rows, width), everyone, 0, 0, tiled=True
    )

    kept, sent = pl.pallas_call(
        mix_kernel,
        out_shape=(
            jax.ShapeDtypeStruct((group_rows, model), F32),
            jax.ShapeDtypeStruct((group_rows, model), BF16),
        ),
        in_specs=in_vmem(3),
        out_specs=in_vmem(2),
        compiler_params=params(8),
        cost_estimate=cost(20_000_000_000),
        name="mix",
    )(sums, hidden_in, out_weight)

    def ring(value, step):
        return lax.ppermute(value, "mp", [(i, (i + step) % mp_count) for i in range(mp_count)])

    steps = mp_count - 1
    arrived = [ring(sent, step) for step in range(1, mp_count)]
    base, *rows = pl.pallas_call(
        lambda *refs: feed_kernel(*refs, steps=steps),
        out_shape=(jax.ShapeDtypeStruct((1, model), F32),)
        + (jax.ShapeDtypeStruct((1, model), BF16),) * steps,
        in_specs=in_vmem(steps + 5),
        out_specs=in_vmem(steps + 1),
        scratch_shapes=[pltpu.VMEM((8, model), F32)],
        compiler_params=params(24),
        name="feed",
    )(kept, *arrived, feed_gain[None], gate_weight, up_weight, down_weight)
    for step, row in enumerate(rows):
        base = base + ring(row, step + 1).astype(F32)
    return (base.astype(BF16), new_entries)


def solution(mesh):
    in_specs = (
        P("pool", None),
        P(),
        P(None, "mp"),
        P(),
        P(),
        P(("pool", "mp"), None, None),
        P(),
        P(),
        P(),
        P("mp", None),
        P(),
        P(None, "mp"),
        P(None, "mp"),
        P("mp", None),
    )
    out_specs = (P(("pool", "mp"), None), P(("pool", "mp"), None))
    return jax.shard_map(shards, mesh=mesh, in_specs=in_specs, out_specs=out_specs, check_vma=False)
```

```python
import jax
import jax.numpy as jnp
import numpy as np
from jax import lax
from jax.experimental import pallas as pl
from jax.experimental.pallas import tpu as pltpu
from jax.sharding import PartitionSpec as P

H = 20
KVH = 5
HD = 64
GROUPS = H // KVH
PAGE = 128
LANES = 128
KEYS = KVH * HD
ENTRY = 2 * KEYS
EPS_WIDE = 1e-05
EPS_HEAD = 1e-06
MIB = 1 << 20

BF16 = jnp.bfloat16
F32 = jnp.float32
I32 = jnp.int32


def up_to(value, step):
    return (value + step - 1) // step * step


def dot(left, right):
    return jnp.dot(left, right, preferred_element_type=F32)


def dot_rows(left, right):
    return lax.dot_general(left, right, (((1,), (1,)), ((), ())), preferred_element_type=F32)


def two_halves(values):
    high = values.astype(BF16)
    return high, (values - high.astype(F32)).astype(BF16)


def lane_iota(shape):
    return lax.broadcasted_iota(I32, shape, len(shape) - 1)


def sublane_iota(shape):
    return lax.broadcasted_iota(I32, shape, len(shape) - 2)


def move_lanes(tile, shift):
    shift %= LANES
    return tile if shift == 0 else pltpu.roll(tile, shift, 1)


def lane_tile(tiles, start, source, step=16):
    spans = []
    for lane in range(0, LANES, step):
        found = source(start + lane)
        piece = None if found is None else (found[0], (lane - found[1]) % LANES)
        if spans and spans[-1][0] == piece:
            spans[-1][2] = lane + step
        else:
            spans.append([piece, lane, lane + step])
    ranges = {}
    for piece, low, high in spans:
        ranges.setdefault(piece, []).append((low, high))
    values = {
        piece: None if piece is None else move_lanes(tiles(piece[0]), piece[1]) for piece in ranges
    }
    like = next(value for value in values.values() if value is not None)
    result = None
    for piece, value in values.items():
        value = jnp.zeros_like(like) if value is None else value
        if result is None:
            result = value
            continue
        lanes = lane_iota(like.shape)
        inside = None
        for low, high in ranges[piece]:
            here = (lanes >= low) & (lanes < high)
            inside = here if inside is None else inside | here
        result = jnp.where(inside, value, result)
    return result


def swap_halves(tile):
    lanes = lane_iota(tile.shape) % HD
    return jnp.where(
        lanes < HD // 2, move_lanes(tile, LANES - HD // 2), move_lanes(tile, HD // 2)
    )


def rms_scale(values, scaling, epsilon):
    mean_square = jnp.mean(values * values, axis=-1, keepdims=True)
    return values * lax.rsqrt(mean_square + epsilon) * scaling


def copy_in(source, target, semaphore):
    copy = pltpu.make_async_copy(source, target, semaphore)
    copy.start()
    return copy


def find_pages(
    table_ref,
    length_ref,
    order_ref,
    frequency_ref,
    query_gain_ref,
    key_gain_ref,
    query_cos_ref,
    query_sin_ref,
    key_cos_ref,
    key_sin_ref,
    row_ref,
    valid_ref,
    pages,
):
    device = lax.axis_index("pool") * lax.axis_size("mp") + lax.axis_index("mp")
    slots = row_ref.shape[0]
    requests, blocks = table_ref.shape
    table = table_ref[...]
    first_page, own_row = device * pages, device
    entry = (sublane_iota(table.shape) * blocks + lane_iota(table.shape) + 1).astype(F32)
    found = [
        jnp.sum(jnp.where(table == first_page + slot, entry, 0.0), axis=0, keepdims=True)
        for slot in range(pages)
    ]
    found.append(jnp.zeros((slots - pages, blocks), F32))
    found = jnp.sum(jnp.concatenate(found, axis=0), axis=1, keepdims=True).astype(I32) - 1
    slot = sublane_iota((slots, 1))
    order = order_ref[...]
    lanes = lane_iota(order.shape)
    own_request = jnp.sum(
        jnp.where(lanes == own_row, order, 0).astype(F32), axis=1, keepdims=True
    ).astype(I32)
    request = jnp.where(slot == pages, own_request, jnp.where(found < 0, -1, found // blocks))
    block = jnp.where(found < 0, 0, found % blocks)
    lane_full = lane_iota((slots, requests))
    length = jnp.sum(
        jnp.where(lane_full == request, length_ref[...].astype(F32), 0.0), axis=1, keepdims=True
    )
    row = jnp.sum(
        jnp.where(order == request, lane_full.astype(F32), 0.0), axis=1, keepdims=True
    ).astype(I32)
    row = jnp.where(request < 0, -1, row)
    valid = jnp.clip(length.astype(I32) - block * PAGE, 0, PAGE)
    valid = jnp.where(slot == pages, 1, jnp.where(request < 0, 0, valid))
    angles = length * frequency_ref[...]
    cosines, sines = jnp.cos(angles), jnp.sin(angles)
    half = lane_iota(angles.shape) % HD
    sines = jnp.where(half < HD // 2, -sines, sines)
    for gain_ref, cos_ref, sin_ref, factor in (
        (query_gain_ref, query_cos_ref, query_sin_ref, HD ** (-0.5)),
        (key_gain_ref, key_cos_ref, key_sin_ref, 1.0),
    ):
        gain = jnp.broadcast_to(gain_ref[...] * factor, (8, HD))
        gain = jnp.concatenate([gain, gain], axis=1)
        cos_ref[...] = cosines * gain[:1]
        sin_ref[...] = sines * swap_halves(gain)[:1]
    row_ref[...] = jnp.broadcast_to(row, row_ref.shape)
    valid_ref[...] = jnp.broadcast_to(valid, valid_ref.shape)


def project_kernel(*refs, pages):
    sources, outputs, rooms, semaphores = refs[:9], refs[9:16], refs[16:25], refs[25]
    rows_ref, gain_ref, weight_ref = rooms[:3]
    out_ref, *found = outputs
    columns = weight_ref.shape[0]
    chunk = up_to(columns // 4, 16)
    first = [copy_in(sources[index], rooms[index], semaphores.at[index]) for index in (0, 1)]
    starts = range(0, columns, chunk)
    copies = []
    for index, start in enumerate(starts):
        part = pl.ds(start, min(chunk, columns - start))
        copies.append(
            copy_in(sources[2].at[part], weight_ref.at[part], semaphores.at[9 + index])
        )
    copies += [
        copy_in(sources[index], rooms[index], semaphores.at[index]) for index in range(3, 9)
    ]
    for copy in first:
        copy.wait()
    normed = rms_scale(rows_ref[...].astype(F32), gain_ref[...], EPS_WIDE).astype(BF16)
    devices, count, padded = out_ref.shape
    if padded > columns:
        out_ref[:, :, columns:] = jnp.zeros((devices, count, padded - columns), BF16)
    for copy in copies:
        copy.wait()
    for start in starts:
        stop = min(start + chunk, columns)
        packed = dot_rows(normed, weight_ref[start:stop])
        out_ref[:, :, start:stop] = jnp.broadcast_to(
            packed.astype(BF16)[None], (devices, count, stop - start)
        )
    find_pages(*rooms[3:], *found, pages)


def attend_kernel(
    packed_ref,
    page_ref,
    query_cos_ref,
    query_sin_ref,
    key_cos_ref,
    key_sin_ref,
    row_ref,
    valid_ref,
    sums_ref,
    entry_ref,
    query_ref,
    fresh_ref,
    partial_ref,
    *,
    pool_count,
    mp_count,
    group_rows,
    columns,
):
    pages = page_ref.shape[0]
    slots = row_ref.shape[0]
    row = row_ref[...][:, :1]
    total_rows = packed_ref.shape[0] * packed_ref.shape[1]
    packed = packed_ref[...].reshape(total_rows, packed_ref.shape[2])
    source = lane_iota((slots, total_rows))
    source_row = source // (mp_count * group_rows) * group_rows + source % group_rows
    source_part = source // group_rows % mp_count
    hit = source_row == row
    choose = jnp.concatenate(
        [jnp.where(hit & (source_part == part), 1.0, 0.0) for part in range(mp_count)], axis=0
    ).astype(BF16)
    chosen = dot(choose, packed)

    def part_tile(key):
        part, tile = key
        return chosen[part * slots : (part + 1) * slots, tile * LANES : (tile + 1) * LANES]

    def part_source(column):
        part, local = divmod(column, columns)
        return (part, local // LANES), local % LANES

    tile_count = (H * HD + ENTRY) // LANES
    query_tiles = H * HD // LANES
    key_tiles = up_to(KEYS, LANES) // LANES
    tiles = [lane_tile(part_tile, t * LANES, part_source) for t in range(tile_count)]
    stacked = jnp.concatenate(tiles[: query_tiles + key_tiles], axis=0)
    ones = jnp.where(
        sublane_iota((LANES, LANES)) // HD == lane_iota((LANES, LANES)) // HD, 1.0, 0.0
    ).astype(BF16)
    high, low = two_halves(stacked * stacked)
    scale = lax.rsqrt((dot(high, ones) + dot(low, ones)) * (1.0 / HD) + EPS_HEAD)
    swapped = swap_halves(stacked)
    split = query_tiles * slots

    def turned(low, high, cos_ref, sin_ref):
        shape = ((high - low) // slots, slots, LANES)
        value = stacked[low:high].reshape(shape) * cos_ref[...][None]
        value = value + swapped[low:high].reshape(shape) * sin_ref[...][None]
        return (value * scale[low:high].reshape(shape)).astype(BF16).astype(F32)

    queries = turned(0, split, query_cos_ref, query_sin_ref)
    keys = turned(split, stacked.shape[0], key_cos_ref, key_sin_ref)
    middle = jnp.where(lane_iota((slots, LANES)) < KEYS % LANES, keys[-1], tiles[-key_tiles])
    entries = [keys[t] for t in range(key_tiles - 1)] + [middle] + tiles[-(key_tiles - 1) :]
    fresh = jnp.concatenate(entries, axis=1)[pages : pages + 8]
    entry_ref[...] = fresh[:1].astype(BF16)
    fresh = jnp.where(sublane_iota(fresh.shape) == 0, fresh, 0.0)
    fresh_ref[...] = jnp.concatenate([fresh, jnp.zeros_like(fresh)], axis=0).astype(BF16)

    wide = key_tiles * LANES
    for member in range(GROUPS):

        def query_source(column):
            kv = column // HD
            if kv >= KVH:
                return None
            head = kv * GROUPS + member
            return head // 2, head % 2 * HD + column % HD

        query_ref[member] = jnp.concatenate(
            [
                lane_tile(lambda t: queries[t], t * LANES, query_source)
                for t in range(key_tiles)
            ],
            axis=1,
        )

    key_mask = lane_iota((8, wide)) // HD == sublane_iota((8, wide))
    value_skip = wide - KEYS
    value_mask = (lane_iota((8, wide)) + (HD - value_skip)) // HD == sublane_iota((8, wide)) + 1
    total_mask = (lane_iota((8, wide)) == sublane_iota((8, wide))) & (
        sublane_iota((8, wide)) < KVH
    )
    value_mask = value_mask & (sublane_iota((8, wide)) < KVH)
    queue = []
    for slot in range(pages + 1):
        spread = jnp.concatenate(
            [
                jnp.where(
                    key_mask,
                    jnp.broadcast_to(query_ref[member, slot : slot + 1, :], (8, wide)),
                    0.0,
                )
                for member in range(GROUPS)
            ],
            axis=0,
        ).astype(BF16)
        key_rows = page_ref[slot, :, :wide] if slot < pages else fresh_ref[:, :wide]
        queue.append(dot_rows(spread, key_rows))
    for slot, scores in enumerate(queue):
        count = valid_ref[slot : slot + 1, : scores.shape[1]]
        weights = jnp.where(lane_iota(scores.shape) < count, jnp.exp(scores), 0.0)
        queue[slot] = weights.astype(BF16), jnp.sum(weights, axis=1, keepdims=True)
    for slot, (weights, totals) in enumerate(queue):
        if slot < pages:
            value_rows = page_ref[slot, :, ENTRY - wide :]
        else:
            value_rows = fresh_ref[:, ENTRY - wide :]
        queue[slot] = dot(weights, value_rows), totals
    for slot, (weighted, totals) in enumerate(queue):
        for member in range(GROUPS):
            low = member * 8
            kept = jnp.where(value_mask, weighted[low : low + 8], 0.0)
            kept = jnp.where(total_mask, totals[low : low + 8], kept)
            partial_ref[member, slot * 8 : slot * 8 + 8, :] = kept

    depth = partial_ref.shape[1]
    spread_row = jnp.sum(
        jnp.where(
            lane_iota((slots, depth)) // 8 == sublane_iota((slots, depth)),
            jnp.broadcast_to(row, (slots, depth)).astype(F32),
            0.0,
        ),
        axis=0,
        keepdims=True,
    ).astype(I32)
    place = sublane_iota((pool_count * 8, depth))
    place = place // 8 * group_rows + place % group_rows
    collect = jnp.where(place == spread_row, 1.0, 0.0).astype(BF16)
    summed = []
    for member in range(GROUPS):
        high, low = two_halves(partial_ref[member])
        summed.append(dot(collect, high) + dot(collect, low))
    first = lane_iota((pool_count * 8, LANES)) < KVH
    totals = None
    for member in range(GROUPS):
        moved = move_lanes(jnp.where(first, summed[member][:, :LANES], 0.0), KVH * member)
        totals = moved if totals is None else totals + moved
    rounded = totals.astype(BF16).astype(F32)
    totals = rounded + move_lanes(totals - rounded, H)

    head_cols = H * HD // mp_count
    width = sums_ref.shape[3]

    def sum_tile(key):
        if key == "totals":
            return totals
        member, tile = key
        return summed[member][:, tile * LANES : (tile + 1) * LANES]

    for part in range(mp_count):

        def sum_source(column):
            if column >= head_cols:
                lane = column - head_cols
                return ("totals", lane) if lane < 2 * H else None
            kv, member = divmod((part * head_cols + column) // HD, GROUPS)
            lane = value_skip + kv * HD + (part * head_cols + column) % HD
            return (member, lane // LANES), lane % LANES

        block = jnp.concatenate(
            [lane_tile(sum_tile, start, sum_source) for start in range(0, width, LANES)], axis=1
        )
        block = block.reshape(pool_count, 8, width)[:, :group_rows]
        sums_ref[:, part] = block.astype(BF16)


def mix_kernel(sums_ref, hidden_ref, weight_ref, kept_ref, sent_ref):
    head_cols = weight_ref.shape[0]
    group_rows = hidden_ref.shape[0]
    part = lax.axis_index("mp")
    sums = jnp.sum(sums_ref[...].astype(F32), axis=0)
    tile = head_cols // LANES * LANES
    totals = sums[:, tile : tile + LANES]
    column = lane_iota((LANES, head_cols)) + part * head_cols
    head = column // HD
    lane = sublane_iota((LANES, head_cols)) - (head_cols - tile)
    index = head % GROUPS * KVH + head // GROUPS
    spread = jnp.where((lane == index) | (lane == index + H), 1.0, 0.0).astype(BF16)
    high = totals.astype(BF16)
    middle, low = two_halves(totals - high.astype(F32))
    denominator = dot(high, spread) + dot(middle, spread) + dot(low, spread)
    attended = (sums[:, :head_cols] / denominator).astype(BF16)
    projected = dot(attended, weight_ref[...])
    kept_ref[...] = projected + hidden_ref[...].astype(F32)
    sent_ref[...] = projected.astype(BF16)


def feed_kernel(*refs, steps):
    kept_ref, *arrived = refs[: steps + 1]
    gain_ref, gate_ref, up_ref, down_ref = refs[steps + 1 : steps + 5]
    base_ref, *sent = refs[steps + 5 : 2 * steps + 6]
    part_ref = refs[-1]
    group_rows = kept_ref.shape[0]
    part = lax.axis_index("mp")
    mixed = kept_ref[...]
    for ref in arrived:
        mixed = mixed + ref[...].astype(F32)
    mixed = mixed.astype(BF16).astype(F32)
    normed = rms_scale(mixed, gain_ref[...], EPS_WIDE).astype(BF16)
    gate = dot(normed, gate_ref[...])
    up = dot(normed, up_ref[...])
    hidden = (gate * jax.nn.sigmoid(gate) * up).astype(BF16)
    part_ref[:group_rows] = dot(hidden, down_ref[...])
    own = part_ref[pl.ds(part, 1), :]
    for step, ref in enumerate(sent):
        target = lax.rem(part + (step + 1), steps + 1)
        ref[...] = part_ref[pl.ds(target, 1), :].astype(BF16)
    part_ref[:group_rows] = mixed
    base_ref[...] = own + part_ref[pl.ds(part, 1), :]


def in_vmem(count):
    return [pl.BlockSpec(memory_space=pltpu.VMEM)] * count


def in_hbm(count):
    return [pl.BlockSpec(memory_space=pltpu.HBM)] * count


def params(limit):
    return pltpu.CompilerParams(vmem_limit_bytes=limit * MIB)


def cost(count):
    return pl.CostEstimate(flops=count, bytes_accessed=0, transcendentals=0)


def like(array):
    return jax.ShapeDtypeStruct(array.shape, array.dtype)


def far(*arrays):
    return [pltpu.with_memory_space_constraint(array, pltpu.HBM) for array in arrays]


def room(array):
    return pltpu.VMEM(array.shape, array.dtype)


def shards(
    hidden_in,
    mix_gain,
    project_in,
    query_gain,
    key_gain,
    page_cache,
    page_table,
    lengths,
    row_order,
    out_weight,
    feed_gain,
    gate_weight,
    up_weight,
    down_weight,
):
    pool_count = lax.axis_size("pool")
    mp_count = lax.axis_size("mp")
    devices = pool_count * mp_count
    group_rows, model = hidden_in.shape
    pages = page_cache.shape[0]
    columns = project_in.shape[1]
    padded = up_to(columns, LANES)
    head_cols = H * HD // mp_count
    width = up_to(head_cols + 2 * H, LANES)
    slots = up_to(pages + 1, 8)
    everyone = ("pool", "mp")
    exponent = np.arange(LANES) % (HD // 2) * (-2.0 / HD)
    frequency = jnp.asarray((10000.0**exponent).astype(np.float32)[None])

    operands = (
        hidden_in,
        mix_gain[None],
        project_in.T,
        page_table,
        lengths[None],
        row_order[None],
        frequency,
        query_gain[None],
        key_gain[None],
    )
    table = jax.ShapeDtypeStruct((slots, LANES), F32)
    index = jax.ShapeDtypeStruct((slots, LANES), I32)
    packed, *found = pl.pallas_call(
        lambda *refs: project_kernel(*refs, pages=pages),
        out_shape=(
            jax.ShapeDtypeStruct((devices, group_rows, padded), BF16),
            table,
            table,
            table,
            table,
            index,
            index,
        ),
        in_specs=in_hbm(9),
        out_specs=in_vmem(7),
        scratch_shapes=[room(x) for x in operands] + [pltpu.SemaphoreType.DMA((16,))],
        compiler_params=params(8),
        cost_estimate=cost(10_000_000_000),
        name="project",
    )(*far(*operands))
    packed = lax.all_to_all(packed, everyone, 0, 0, tiled=True)

    wide = up_to(KEYS, LANES)
    sums, new_entries = pl.pallas_call(
        lambda *refs: attend_kernel(
            *refs,
            pool_count=pool_count,
            mp_count=mp_count,
            group_rows=group_rows,
            columns=columns,
        ),
        out_shape=(
            jax.ShapeDtypeStruct((pool_count, mp_count, group_rows, width), BF16),
            jax.ShapeDtypeStruct((1, ENTRY), BF16),
        ),
        in_specs=in_vmem(8),
        out_specs=in_vmem(2),
        scratch_shapes=[
            pltpu.VMEM((GROUPS, slots, wide), F32),
            pltpu.VMEM((16, ENTRY), BF16),
            pltpu.VMEM((GROUPS, (pages + 1) * 8, wide), F32),
        ],
        compiler_params=params(16),
        cost_estimate=cost(20_000_000_000),
        name="attend",
    )(
        packed,
        page_cache,
        *found,
    )
    sums = lax.all_to_all(
        sums.reshape(devices, group_rows, width), everyone, 0, 0, tiled=True
    )

    kept, sent = pl.pallas_call(
        mix_kernel,
        out_shape=(
            jax.ShapeDtypeStruct((group_rows, model), F32),
            jax.ShapeDtypeStruct((group_rows, model), BF16),
        ),
        in_specs=in_vmem(3),
        out_specs=in_vmem(2),
        compiler_params=params(8),
        cost_estimate=cost(20_000_000_000),
        name="mix",
    )(sums, hidden_in, out_weight)

    def ring(value, step):
        return lax.ppermute(value, "mp", [(i, (i + step) % mp_count) for i in range(mp_count)])

    steps = mp_count - 1
    arrived = [ring(sent, step) for step in range(1, mp_count)]
    base, *rows = pl.pallas_call(
        lambda *refs: feed_kernel(*refs, steps=steps),
        out_shape=(jax.ShapeDtypeStruct((1, model), F32),)
        + (jax.ShapeDtypeStruct((1, model), BF16),) * steps,
        in_specs=in_vmem(steps + 5),
        out_specs=in_vmem(steps + 1),
        scratch_shapes=[pltpu.VMEM((8, model), F32)],
        compiler_params=params(24),
        name="feed",
    )(kept, *arrived, feed_gain[None], gate_weight, up_weight, down_weight)
    for step, row in enumerate(rows):
        base = base + ring(row, step + 1).astype(F32)
    return (base.astype(BF16), new_entries)


def solution(mesh):
    in_specs = (
        P("pool", None),
        P(),
        P(None, "mp"),
        P(),
        P(),
        P(("pool", "mp"), None, None),
        P(),
        P(),
        P(),
        P("mp", None),
        P(),
        P(None, "mp"),
        P(None, "mp"),
        P("mp", None),
    )
    out_specs = (P(("pool", "mp"), None), P(("pool", "mp"), None))
    return jax.shard_map(shards, mesh=mesh, in_specs=in_specs, out_specs=out_specs, check_vma=False)
```

```python
import jax
import jax.numpy as jnp
import numpy as np
from jax import lax
from jax.experimental import pallas as pl
from jax.experimental.pallas import tpu as pltpu
from jax.sharding import PartitionSpec as P

H = 20
KVH = 5
HD = 64
GROUPS = H // KVH
PAGE = 128
LANES = 128
KEYS = KVH * HD
ENTRY = 2 * KEYS
EPS_WIDE = 1e-05
EPS_HEAD = 1e-06
MIB = 1 << 20

BF16 = jnp.bfloat16
F32 = jnp.float32
I32 = jnp.int32


def up_to(value, step):
    return (value + step - 1) // step * step


def dot(left, right):
    return jnp.dot(left, right, preferred_element_type=F32)


def dot_rows(left, right):
    return lax.dot_general(left, right, (((1,), (1,)), ((), ())), preferred_element_type=F32)


def two_halves(values):
    high = values.astype(BF16)
    return high, (values - high.astype(F32)).astype(BF16)


def lane_iota(shape):
    return lax.broadcasted_iota(I32, shape, len(shape) - 1)


def sublane_iota(shape):
    return lax.broadcasted_iota(I32, shape, len(shape) - 2)


def move_lanes(tile, shift):
    shift %= LANES
    return tile if shift == 0 else pltpu.roll(tile, shift, 1)


def lane_tile(tiles, start, source, step=16):
    spans = []
    for lane in range(0, LANES, step):
        found = source(start + lane)
        piece = None if found is None else (found[0], (lane - found[1]) % LANES)
        if spans and spans[-1][0] == piece:
            spans[-1][2] = lane + step
        else:
            spans.append([piece, lane, lane + step])
    ranges = {}
    for piece, low, high in spans:
        ranges.setdefault(piece, []).append((low, high))
    values = {
        piece: None if piece is None else move_lanes(tiles(piece[0]), piece[1]) for piece in ranges
    }
    like = next(value for value in values.values() if value is not None)
    result = None
    for piece, value in values.items():
        value = jnp.zeros_like(like) if value is None else value
        if result is None:
            result = value
            continue
        lanes = lane_iota(like.shape)
        inside = None
        for low, high in ranges[piece]:
            here = (lanes >= low) & (lanes < high)
            inside = here if inside is None else inside | here
        result = jnp.where(inside, value, result)
    return result


def swap_halves(tile):
    lanes = lane_iota(tile.shape) % HD
    return jnp.where(
        lanes < HD // 2, move_lanes(tile, LANES - HD // 2), move_lanes(tile, HD // 2)
    )


def rms_scale(values, scaling, epsilon):
    mean_square = jnp.mean(values * values, axis=-1, keepdims=True)
    return values * lax.rsqrt(mean_square + epsilon) * scaling


def copy_in(source, target, semaphore):
    copy = pltpu.make_async_copy(source, target, semaphore)
    copy.start()
    return copy


def find_pages(
    table_ref,
    length_ref,
    order_ref,
    frequency_ref,
    query_gain_ref,
    key_gain_ref,
    query_cos_ref,
    query_sin_ref,
    key_cos_ref,
    key_sin_ref,
    row_ref,
    valid_ref,
    pages,
):
    device = lax.axis_index("pool") * lax.axis_size("mp") + lax.axis_index("mp")
    slots = row_ref.shape[0]
    requests, blocks = table_ref.shape
    table = table_ref[...]
    first_page, own_row = device * pages, device
    entry = (sublane_iota(table.shape) * blocks + lane_iota(table.shape) + 1).astype(F32)
    found = [
        jnp.sum(jnp.where(table == first_page + slot, entry, 0.0), axis=0, keepdims=True)
        for slot in range(pages)
    ]
    found.append(jnp.zeros((slots - pages, blocks), F32))
    found = jnp.sum(jnp.concatenate(found, axis=0), axis=1, keepdims=True).astype(I32) - 1
    slot = sublane_iota((slots, 1))
    order = order_ref[...]
    lanes = lane_iota(order.shape)
    own_request = jnp.sum(
        jnp.where(lanes == own_row, order, 0).astype(F32), axis=1, keepdims=True
    ).astype(I32)
    request = jnp.where(slot == pages, own_request, jnp.where(found < 0, -1, found // blocks))
    block = jnp.where(found < 0, 0, found % blocks)
    lane_full = lane_iota((slots, requests))
    length = jnp.sum(
        jnp.where(lane_full == request, length_ref[...].astype(F32), 0.0), axis=1, keepdims=True
    )
    row = jnp.sum(
        jnp.where(order == request, lane_full.astype(F32), 0.0), axis=1, keepdims=True
    ).astype(I32)
    row = jnp.where(request < 0, -1, row)
    valid = jnp.clip(length.astype(I32) - block * PAGE, 0, PAGE)
    valid = jnp.where(slot == pages, 1, jnp.where(request < 0, 0, valid))
    angles = length * frequency_ref[...]
    cosines, sines = jnp.cos(angles), jnp.sin(angles)
    half = lane_iota(angles.shape) % HD
    sines = jnp.where(half < HD // 2, -sines, sines)
    for gain_ref, cos_ref, sin_ref, factor in (
        (query_gain_ref, query_cos_ref, query_sin_ref, HD ** (-0.5)),
        (key_gain_ref, key_cos_ref, key_sin_ref, 1.0),
    ):
        gain = jnp.broadcast_to(gain_ref[...] * factor, (8, HD))
        gain = jnp.concatenate([gain, gain], axis=1)
        cos_ref[...] = cosines * gain[:1]
        sin_ref[...] = sines * swap_halves(gain)[:1]
    row_ref[...] = jnp.broadcast_to(row, row_ref.shape)
    valid_ref[...] = jnp.broadcast_to(valid, valid_ref.shape)


def project_kernel(*refs, pages):
    sources, outputs, rooms, semaphores = refs[:9], refs[9:16], refs[16:25], refs[25]
    rows_ref, gain_ref, weight_ref = rooms[:3]
    out_ref, *found = outputs
    columns = weight_ref.shape[0]
    chunk = up_to(columns // 4, 16)
    first = [copy_in(sources[index], rooms[index], semaphores.at[index]) for index in (0, 1)]
    starts = range(0, columns, chunk)
    copies = []
    for index, start in enumerate(starts):
        part = pl.ds(start, min(chunk, columns - start))
        copies.append(
            copy_in(sources[2].at[part], weight_ref.at[part], semaphores.at[9 + index])
        )
    copies += [
        copy_in(sources[index], rooms[index], semaphores.at[index]) for index in range(3, 9)
    ]
    for copy in first:
        copy.wait()
    normed = rms_scale(rows_ref[...].astype(F32), gain_ref[...], EPS_WIDE).astype(BF16)
    devices, count, padded = out_ref.shape
    if padded > columns:
        out_ref[:, :, columns:] = jnp.zeros((devices, count, padded - columns), BF16)
    for copy in copies:
        copy.wait()
    for start in starts:
        stop = min(start + chunk, columns)
        packed = dot_rows(normed, weight_ref[start:stop])
        out_ref[:, :, start:stop] = jnp.broadcast_to(
            packed.astype(BF16)[None], (devices, count, stop - start)
        )
    find_pages(*rooms[3:], *found, pages)


def attend_kernel(
    packed_ref,
    page_ref,
    query_cos_ref,
    query_sin_ref,
    key_cos_ref,
    key_sin_ref,
    row_ref,
    valid_ref,
    sums_ref,
    entry_ref,
    query_ref,
    fresh_ref,
    partial_ref,
    *,
    pool_count,
    mp_count,
    group_rows,
    columns,
):
    pages = page_ref.shape[0]
    slots = row_ref.shape[0]
    row = row_ref[...][:, :1]
    total_rows = packed_ref.shape[0] * packed_ref.shape[1]
    packed = packed_ref[...].reshape(total_rows, packed_ref.shape[2])
    source = lane_iota((slots, total_rows))
    source_row = source // (mp_count * group_rows) * group_rows + source % group_rows
    source_part = source // group_rows % mp_count
    hit = source_row == row
    choose = jnp.concatenate(
        [jnp.where(hit & (source_part == part), 1.0, 0.0) for part in range(mp_count)], axis=0
    ).astype(BF16)
    chosen = dot(choose, packed)

    def part_tile(key):
        part, tile = key
        return chosen[part * slots : (part + 1) * slots, tile * LANES : (tile + 1) * LANES]

    def part_source(column):
        part, local = divmod(column, columns)
        return (part, local // LANES), local % LANES

    tile_count = (H * HD + ENTRY) // LANES
    query_tiles = H * HD // LANES
    key_tiles = up_to(KEYS, LANES) // LANES
    tiles = [lane_tile(part_tile, t * LANES, part_source) for t in range(tile_count)]
    stacked = jnp.concatenate(tiles[: query_tiles + key_tiles], axis=0)
    ones = jnp.where(
        sublane_iota((LANES, LANES)) // HD == lane_iota((LANES, LANES)) // HD, 1.0, 0.0
    ).astype(BF16)
    high, low = two_halves(stacked * stacked)
    scale = lax.rsqrt((dot(high, ones) + dot(low, ones)) * (1.0 / HD) + EPS_HEAD)
    swapped = swap_halves(stacked)
    split = query_tiles * slots

    def turned(low, high, cos_ref, sin_ref):
        shape = ((high - low) // slots, slots, LANES)
        value = stacked[low:high].reshape(shape) * cos_ref[...][None]
        value = value + swapped[low:high].reshape(shape) * sin_ref[...][None]
        return (value * scale[low:high].reshape(shape)).astype(BF16).astype(F32)

    queries = turned(0, split, query_cos_ref, query_sin_ref)
    keys = turned(split, stacked.shape[0], key_cos_ref, key_sin_ref)
    middle = jnp.where(lane_iota((slots, LANES)) < KEYS % LANES, keys[-1], tiles[-key_tiles])
    entries = [keys[t] for t in range(key_tiles - 1)] + [middle] + tiles[-(key_tiles - 1) :]
    fresh = jnp.concatenate(entries, axis=1)[pages : pages + 8]
    entry_ref[...] = fresh[:1].astype(BF16)
    fresh = jnp.where(sublane_iota(fresh.shape) == 0, fresh, 0.0)
    fresh_ref[...] = jnp.concatenate([fresh, jnp.zeros_like(fresh)], axis=0).astype(BF16)

    wide = key_tiles * LANES
    for member in range(GROUPS):

        def query_source(column):
            kv = column // HD
            if kv >= KVH:
                return None
            head = kv * GROUPS + member
            return head // 2, head % 2 * HD + column % HD

        query_ref[member] = jnp.concatenate(
            [
                lane_tile(lambda t: queries[t], t * LANES, query_source)
                for t in range(key_tiles)
            ],
            axis=1,
        )

    key_mask = lane_iota((8, wide)) // HD == sublane_iota((8, wide))
    value_skip = wide - KEYS
    value_mask = (lane_iota((8, wide)) + (HD - value_skip)) // HD == sublane_iota((8, wide)) + 1
    total_mask = (lane_iota((8, wide)) == sublane_iota((8, wide))) & (
        sublane_iota((8, wide)) < KVH
    )
    value_mask = value_mask & (sublane_iota((8, wide)) < KVH)
    queue = []
    for slot in range(pages + 1):
        spread = jnp.concatenate(
            [
                jnp.where(
                    key_mask,
                    jnp.broadcast_to(query_ref[member, slot : slot + 1, :], (8, wide)),
                    0.0,
                )
                for member in range(GROUPS)
            ],
            axis=0,
        ).astype(BF16)
        key_rows = page_ref[slot, :, :wide] if slot < pages else fresh_ref[:, :wide]
        queue.append(dot_rows(spread, key_rows))
    for slot, scores in enumerate(queue):
        count = valid_ref[slot : slot + 1, : scores.shape[1]]
        weights = jnp.where(lane_iota(scores.shape) < count, jnp.exp(scores), 0.0)
        queue[slot] = weights.astype(BF16), jnp.sum(weights, axis=1, keepdims=True)
    for slot, (weights, totals) in enumerate(queue):
        if slot < pages:
            value_rows = page_ref[slot, :, ENTRY - wide :]
        else:
            value_rows = fresh_ref[:, ENTRY - wide :]
        queue[slot] = dot(weights, value_rows), totals
    for slot, (weighted, totals) in enumerate(queue):
        for member in range(GROUPS):
            low = member * 8
            kept = jnp.where(value_mask, weighted[low : low + 8], 0.0)
            kept = jnp.where(total_mask, totals[low : low + 8], kept)
            partial_ref[member, slot * 8 : slot * 8 + 8, :] = kept

    depth = partial_ref.shape[1]
    spread_row = jnp.sum(
        jnp.where(
            lane_iota((slots, depth)) // 8 == sublane_iota((slots, depth)),
            jnp.broadcast_to(row, (slots, depth)).astype(F32),
            0.0,
        ),
        axis=0,
        keepdims=True,
    ).astype(I32)
    place = sublane_iota((pool_count * 8, depth))
    place = place // 8 * group_rows + place % group_rows
    collect = jnp.where(place == spread_row, 1.0, 0.0).astype(BF16)
    summed = []
    for member in range(GROUPS):
        high, low = two_halves(partial_ref[member])
        summed.append(dot(collect, high) + dot(collect, low))
    first = lane_iota((pool_count * 8, LANES)) < KVH
    totals = None
    for member in range(GROUPS):
        moved = move_lanes(jnp.where(first, summed[member][:, :LANES], 0.0), KVH * member)
        totals = moved if totals is None else totals + moved
    rounded = totals.astype(BF16).astype(F32)
    totals = rounded + move_lanes(totals - rounded, H)

    head_cols = H * HD // mp_count
    width = sums_ref.shape[3]

    def sum_tile(key):
        if key == "totals":
            return totals
        member, tile = key
        return summed[member][:, tile * LANES : (tile + 1) * LANES]

    for part in range(mp_count):

        def sum_source(column):
            if column >= head_cols:
                lane = column - head_cols
                return ("totals", lane) if lane < 2 * H else None
            kv, member = divmod((part * head_cols + column) // HD, GROUPS)
            lane = value_skip + kv * HD + (part * head_cols + column) % HD
            return (member, lane // LANES), lane % LANES

        block = jnp.concatenate(
            [lane_tile(sum_tile, start, sum_source) for start in range(0, width, LANES)], axis=1
        )
        block = block.reshape(pool_count, 8, width)[:, :group_rows]
        sums_ref[:, part] = block.astype(BF16)


def mix_kernel(sums_ref, hidden_ref, weight_ref, kept_ref, sent_ref):
    head_cols = weight_ref.shape[0]
    group_rows = hidden_ref.shape[0]
    part = lax.axis_index("mp")
    sums = jnp.sum(sums_ref[...].astype(F32), axis=0)
    tile = head_cols // LANES * LANES
    totals = sums[:, tile : tile + LANES]
    column = lane_iota((LANES, head_cols)) + part * head_cols
    head = column // HD
    lane = sublane_iota((LANES, head_cols)) - (head_cols - tile)
    index = head % GROUPS * KVH + head // GROUPS
    spread = jnp.where((lane == index) | (lane == index + H), 1.0, 0.0).astype(BF16)
    high = totals.astype(BF16)
    middle, low = two_halves(totals - high.astype(F32))
    denominator = dot(high, spread) + dot(middle, spread) + dot(low, spread)
    attended = (sums[:, :head_cols] / denominator).astype(BF16)
    projected = dot(attended, weight_ref[...])
    kept_ref[...] = projected + hidden_ref[...].astype(F32)
    sent_ref[...] = projected.astype(BF16)


def feed_kernel(*refs, steps):
    kept_ref, *arrived = refs[: steps + 1]
    gain_ref, gate_ref, up_ref, down_ref = refs[steps + 1 : steps + 5]
    base_ref, *sent = refs[steps + 5 : 2 * steps + 6]
    part_ref = refs[-1]
    group_rows = kept_ref.shape[0]
    part = lax.axis_index("mp")
    mixed = kept_ref[...]
    for ref in arrived:
        mixed = mixed + ref[...].astype(F32)
    mixed = mixed.astype(BF16).astype(F32)
    normed = rms_scale(mixed, gain_ref[...], EPS_WIDE).astype(BF16)
    gate = dot(normed, gate_ref[...])
    up = dot(normed, up_ref[...])
    hidden = (gate * jax.nn.sigmoid(gate) * up).astype(BF16)
    part_ref[:group_rows] = dot(hidden, down_ref[...])
    own = part_ref[pl.ds(part, 1), :]
    for step, ref in enumerate(sent):
        target = lax.rem(part + (step + 1), steps + 1)
        ref[...] = part_ref[pl.ds(target, 1), :].astype(BF16)
    part_ref[:group_rows] = mixed
    base_ref[...] = own + part_ref[pl.ds(part, 1), :]


def in_vmem(count):
    return [pl.BlockSpec(memory_space=pltpu.VMEM)] * count


def in_hbm(count):
    return [pl.BlockSpec(memory_space=pltpu.HBM)] * count


def params(limit):
    return pltpu.CompilerParams(vmem_limit_bytes=limit * MIB)


def cost(count):
    return pl.CostEstimate(flops=count, bytes_accessed=0, transcendentals=0)


def like(array):
    return jax.ShapeDtypeStruct(array.shape, array.dtype)


def far(*arrays):
    return [pltpu.with_memory_space_constraint(array, pltpu.HBM) for array in arrays]


def room(array):
    return pltpu.VMEM(array.shape, array.dtype)


def shards(
    hidden_in,
    mix_gain,
    project_in,
    query_gain,
    key_gain,
    page_cache,
    page_table,
    lengths,
    row_order,
    out_weight,
    feed_gain,
    gate_weight,
    up_weight,
    down_weight,
):
    pool_count = lax.axis_size("pool")
    mp_count = lax.axis_size("mp")
    devices = pool_count * mp_count
    group_rows, model = hidden_in.shape
    pages = page_cache.shape[0]
    columns = project_in.shape[1]
    padded = up_to(columns, LANES)
    head_cols = H * HD // mp_count
    width = up_to(head_cols + 2 * H, LANES)
    slots = up_to(pages + 1, 8)
    everyone = ("pool", "mp")
    exponent = np.arange(LANES) % (HD // 2) * (-2.0 / HD)
    frequency = jnp.asarray((10000.0**exponent).astype(np.float32)[None])

    operands = (
        hidden_in,
        mix_gain[None],
        project_in.T,
        page_table,
        lengths[None],
        row_order[None],
        frequency,
        query_gain[None],
        key_gain[None],
    )
    table = jax.ShapeDtypeStruct((slots, LANES), F32)
    index = jax.ShapeDtypeStruct((slots, LANES), I32)
    packed, *found = pl.pallas_call(
        lambda *refs: project_kernel(*refs, pages=pages),
        out_shape=(
            jax.ShapeDtypeStruct((devices, group_rows, padded), BF16),
            table,
            table,
            table,
            table,
            index,
            index,
        ),
        in_specs=in_hbm(9),
        out_specs=in_vmem(7),
        scratch_shapes=[room(x) for x in operands] + [pltpu.SemaphoreType.DMA((16,))],
        compiler_params=params(8),
        cost_estimate=cost(10_000_000_000),
        name="project",
    )(*far(*operands))
    packed = lax.all_to_all(packed, everyone, 0, 0, tiled=True)

    wide = up_to(KEYS, LANES)
    sums, new_entries = pl.pallas_call(
        lambda *refs: attend_kernel(
            *refs,
            pool_count=pool_count,
            mp_count=mp_count,
            group_rows=group_rows,
            columns=columns,
        ),
        out_shape=(
            jax.ShapeDtypeStruct((pool_count, mp_count, group_rows, width), BF16),
            jax.ShapeDtypeStruct((1, ENTRY), BF16),
        ),
        in_specs=in_vmem(8),
        out_specs=in_vmem(2),
        scratch_shapes=[
            pltpu.VMEM((GROUPS, slots, wide), F32),
            pltpu.VMEM((16, ENTRY), BF16),
            pltpu.VMEM((GROUPS, (pages + 1) * 8, wide), F32),
        ],
        compiler_params=params(16),
        cost_estimate=cost(20_000_000_000),
        name="attend",
    )(
        packed,
        page_cache,
        *found,
    )
    sums = lax.all_to_all(
        sums.reshape(devices, group_rows, width), everyone, 0, 0, tiled=True
    )

    kept, sent = pl.pallas_call(
        mix_kernel,
        out_shape=(
            jax.ShapeDtypeStruct((group_rows, model), F32),
            jax.ShapeDtypeStruct((group_rows, model), BF16),
        ),
        in_specs=in_vmem(3),
        out_specs=in_vmem(2),
        compiler_params=params(8),
        cost_estimate=cost(20_000_000_000),
        name="mix",
    )(sums, hidden_in, out_weight)

    def ring(value, step):
        return lax.ppermute(value, "mp", [(i, (i + step) % mp_count) for i in range(mp_count)])

    def swap(value, step):
        if mp_count & (mp_count - 1):
            return ring(value, step)
        step ^= step >> 1
        return lax.ppermute(value, "mp", [(i, i ^ step) for i in range(mp_count)])

    steps = mp_count - 1
    arrived = [swap(sent, step) for step in range(1, mp_count)]
    base, *rows = pl.pallas_call(
        lambda *refs: feed_kernel(*refs, steps=steps),
        out_shape=(jax.ShapeDtypeStruct((1, model), F32),)
        + (jax.ShapeDtypeStruct((1, model), BF16),) * steps,
        in_specs=in_vmem(steps + 5),
        out_specs=in_vmem(steps + 1),
        scratch_shapes=[pltpu.VMEM((8, model), F32)],
        compiler_params=params(24),
        name="feed",
    )(kept, *arrived, feed_gain[None], gate_weight, up_weight, down_weight)
    for step, row in enumerate(rows):
        base = base + ring(row, step + 1).astype(F32)
    return (base.astype(BF16), new_entries)


def solution(mesh):
    in_specs = (
        P("pool", None),
        P(),
        P(None, "mp"),
        P(),
        P(),
        P(("pool", "mp"), None, None),
        P(),
        P(),
        P(),
        P("mp", None),
        P(),
        P(None, "mp"),
        P(None, "mp"),
        P("mp", None),
    )
    out_specs = (P(("pool", "mp"), None), P(("pool", "mp"), None))
    return jax.shard_map(shards, mesh=mesh, in_specs=in_specs, out_specs=out_specs, check_vma=False)
```

```python
import jax
import jax.numpy as jnp
import numpy as np
from jax import lax
from jax.experimental import pallas as pl
from jax.experimental.pallas import tpu as pltpu
from jax.sharding import PartitionSpec as P

H = 20
KVH = 5
HD = 64
GROUPS = H // KVH
PAGE = 128
LANES = 128
KEYS = KVH * HD
ENTRY = 2 * KEYS
EPS_WIDE = 1e-05
EPS_HEAD = 1e-06
MIB = 1 << 20

BF16 = jnp.bfloat16
F32 = jnp.float32
I32 = jnp.int32


def up_to(value, step):
    return (value + step - 1) // step * step


def dot(left, right):
    return jnp.dot(left, right, preferred_element_type=F32)


def dot_rows(left, right):
    return lax.dot_general(left, right, (((1,), (1,)), ((), ())), preferred_element_type=F32)


def two_halves(values):
    high = values.astype(BF16)
    return high, (values - high.astype(F32)).astype(BF16)


def lane_iota(shape):
    return lax.broadcasted_iota(I32, shape, len(shape) - 1)


def sublane_iota(shape):
    return lax.broadcasted_iota(I32, shape, len(shape) - 2)


def move_lanes(tile, shift):
    shift %= LANES
    return tile if shift == 0 else pltpu.roll(tile, shift, 1)


def lane_tile(tiles, start, source, step=16):
    spans = []
    for lane in range(0, LANES, step):
        found = source(start + lane)
        piece = None if found is None else (found[0], (lane - found[1]) % LANES)
        if spans and spans[-1][0] == piece:
            spans[-1][2] = lane + step
        else:
            spans.append([piece, lane, lane + step])
    ranges = {}
    for piece, low, high in spans:
        ranges.setdefault(piece, []).append((low, high))
    values = {
        piece: None if piece is None else move_lanes(tiles(piece[0]), piece[1]) for piece in ranges
    }
    like = next(value for value in values.values() if value is not None)
    result = None
    for piece, value in values.items():
        value = jnp.zeros_like(like) if value is None else value
        if result is None:
            result = value
            continue
        lanes = lane_iota(like.shape)
        inside = None
        for low, high in ranges[piece]:
            here = (lanes >= low) & (lanes < high)
            inside = here if inside is None else inside | here
        result = jnp.where(inside, value, result)
    return result


def swap_halves(tile):
    lanes = lane_iota(tile.shape) % HD
    return jnp.where(
        lanes < HD // 2, move_lanes(tile, LANES - HD // 2), move_lanes(tile, HD // 2)
    )


def rms_scale(values, scaling, epsilon):
    mean_square = jnp.mean(values * values, axis=-1, keepdims=True)
    return values * lax.rsqrt(mean_square + epsilon) * scaling


def copy_in(source, target, semaphore):
    copy = pltpu.make_async_copy(source, target, semaphore)
    copy.start()
    return copy


def find_pages(
    table_ref,
    length_ref,
    order_ref,
    frequency_ref,
    query_gain_ref,
    key_gain_ref,
    query_cos_ref,
    query_sin_ref,
    key_cos_ref,
    key_sin_ref,
    row_ref,
    valid_ref,
    pages,
):
    device = lax.axis_index("pool") * lax.axis_size("mp") + lax.axis_index("mp")
    slots = row_ref.shape[0]
    requests, blocks = table_ref.shape
    table = table_ref[...]
    first_page, own_row = device * pages, device
    entry = (sublane_iota(table.shape) * blocks + lane_iota(table.shape) + 1).astype(F32)
    found = [
        jnp.sum(jnp.where(table == first_page + slot, entry, 0.0), axis=0, keepdims=True)
        for slot in range(pages)
    ]
    found.append(jnp.zeros((slots - pages, blocks), F32))
    found = jnp.sum(jnp.concatenate(found, axis=0), axis=1, keepdims=True).astype(I32) - 1
    slot = sublane_iota((slots, 1))
    order = order_ref[...]
    lanes = lane_iota(order.shape)
    own_request = jnp.sum(
        jnp.where(lanes == own_row, order, 0).astype(F32), axis=1, keepdims=True
    ).astype(I32)
    request = jnp.where(slot == pages, own_request, jnp.where(found < 0, -1, found // blocks))
    block = jnp.where(found < 0, 0, found % blocks)
    lane_full = lane_iota((slots, requests))
    length = jnp.sum(
        jnp.where(lane_full == request, length_ref[...].astype(F32), 0.0), axis=1, keepdims=True
    )
    row = jnp.sum(
        jnp.where(order == request, lane_full.astype(F32), 0.0), axis=1, keepdims=True
    ).astype(I32)
    row = jnp.where(request < 0, -1, row)
    valid = jnp.clip(length.astype(I32) - block * PAGE, 0, PAGE)
    valid = jnp.where(slot == pages, 1, jnp.where(request < 0, 0, valid))
    angles = length * frequency_ref[...]
    cosines, sines = jnp.cos(angles), jnp.sin(angles)
    half = lane_iota(angles.shape) % HD
    sines = jnp.where(half < HD // 2, -sines, sines)
    for gain_ref, cos_ref, sin_ref, factor in (
        (query_gain_ref, query_cos_ref, query_sin_ref, HD ** (-0.5)),
        (key_gain_ref, key_cos_ref, key_sin_ref, 1.0),
    ):
        gain = jnp.broadcast_to(gain_ref[...] * factor, (8, HD))
        gain = jnp.concatenate([gain, gain], axis=1)
        cos_ref[...] = cosines * gain[:1]
        sin_ref[...] = sines * swap_halves(gain)[:1]
    row_ref[...] = jnp.broadcast_to(row, row_ref.shape)
    valid_ref[...] = jnp.broadcast_to(valid, valid_ref.shape)


def project_kernel(*refs, pages):
    sources, outputs, rooms, semaphores = refs[:9], refs[9:16], refs[16:25], refs[25]
    rows_ref, gain_ref, weight_ref = rooms[:3]
    out_ref, *found = outputs
    columns = weight_ref.shape[0]
    chunk = up_to(columns // 4, 16)
    first = [copy_in(sources[index], rooms[index], semaphores.at[index]) for index in (0, 1)]
    starts = range(0, columns, chunk)
    copies = []
    for index, start in enumerate(starts):
        part = pl.ds(start, min(chunk, columns - start))
        copies.append(
            copy_in(sources[2].at[part], weight_ref.at[part], semaphores.at[9 + index])
        )
    copies += [
        copy_in(sources[index], rooms[index], semaphores.at[index]) for index in range(3, 9)
    ]
    for copy in first:
        copy.wait()
    normed = rms_scale(rows_ref[...].astype(F32), gain_ref[...], EPS_WIDE).astype(BF16)
    devices, count, padded = out_ref.shape
    if padded > columns:
        out_ref[:, :, columns:] = jnp.zeros((devices, count, padded - columns), BF16)
    for copy in copies:
        copy.wait()
    for start in starts:
        stop = min(start + chunk, columns)
        packed = dot_rows(normed, weight_ref[start:stop])
        out_ref[:, :, start:stop] = jnp.broadcast_to(
            packed.astype(BF16)[None], (devices, count, stop - start)
        )
    find_pages(*rooms[3:], *found, pages)


def attend_kernel(
    packed_ref,
    page_ref,
    query_cos_ref,
    query_sin_ref,
    key_cos_ref,
    key_sin_ref,
    row_ref,
    valid_ref,
    sums_ref,
    entry_ref,
    query_ref,
    fresh_ref,
    partial_ref,
    *,
    pool_count,
    mp_count,
    group_rows,
    columns,
):
    pages = page_ref.shape[0]
    slots = row_ref.shape[0]
    row = row_ref[...][:, :1]
    total_rows = packed_ref.shape[0] * packed_ref.shape[1]
    packed = packed_ref[...].reshape(total_rows, packed_ref.shape[2])
    source = lane_iota((slots, total_rows))
    source_row = source // (mp_count * group_rows) * group_rows + source % group_rows
    source_part = source // group_rows % mp_count
    hit = source_row == row
    choose = jnp.concatenate(
        [jnp.where(hit & (source_part == part), 1.0, 0.0) for part in range(mp_count)], axis=0
    ).astype(BF16)
    chosen = dot(choose, packed)

    def part_tile(key):
        part, tile = key
        return chosen[part * slots : (part + 1) * slots, tile * LANES : (tile + 1) * LANES]

    def part_source(column):
        part, local = divmod(column, columns)
        return (part, local // LANES), local % LANES

    tile_count = (H * HD + ENTRY) // LANES
    query_tiles = H * HD // LANES
    key_tiles = up_to(KEYS, LANES) // LANES
    tiles = [lane_tile(part_tile, t * LANES, part_source) for t in range(tile_count)]
    stacked = jnp.concatenate(tiles[: query_tiles + key_tiles], axis=0)
    ones = jnp.where(
        sublane_iota((2 * LANES, LANES)) % LANES // HD == lane_iota((2 * LANES, LANES)) // HD,
        1.0,
        0.0,
    ).astype(BF16)
    squares = jnp.concatenate(two_halves(stacked * stacked), axis=1)
    scale = lax.rsqrt(dot(squares, ones) * (1.0 / HD) + EPS_HEAD)
    swapped = swap_halves(stacked)
    split = query_tiles * slots

    def turned(low, high, cos_ref, sin_ref):
        shape = ((high - low) // slots, slots, LANES)
        value = stacked[low:high].reshape(shape) * cos_ref[...][None]
        value = value + swapped[low:high].reshape(shape) * sin_ref[...][None]
        return (value * scale[low:high].reshape(shape)).astype(BF16).astype(F32)

    queries = turned(0, split, query_cos_ref, query_sin_ref)
    keys = turned(split, stacked.shape[0], key_cos_ref, key_sin_ref)
    middle = jnp.where(lane_iota((slots, LANES)) < KEYS % LANES, keys[-1], tiles[-key_tiles])
    entries = [keys[t] for t in range(key_tiles - 1)] + [middle] + tiles[-(key_tiles - 1) :]
    fresh = jnp.concatenate(entries, axis=1)[pages : pages + 8]
    entry_ref[...] = fresh[:1].astype(BF16)
    fresh = jnp.where(sublane_iota(fresh.shape) == 0, fresh, 0.0)
    fresh_ref[...] = jnp.concatenate([fresh, jnp.zeros_like(fresh)], axis=0).astype(BF16)

    wide = key_tiles * LANES
    for member in range(GROUPS):

        def query_source(column):
            kv = column // HD
            if kv >= KVH:
                return None
            head = kv * GROUPS + member
            return head // 2, head % 2 * HD + column % HD

        query_ref[member] = jnp.concatenate(
            [
                lane_tile(lambda t: queries[t], t * LANES, query_source)
                for t in range(key_tiles)
            ],
            axis=1,
        )

    key_mask = lane_iota((8, wide)) // HD == sublane_iota((8, wide))
    value_skip = wide - KEYS
    value_mask = (lane_iota((8, wide)) + (HD - value_skip)) // HD == sublane_iota((8, wide)) + 1
    total_mask = (lane_iota((8, wide)) == sublane_iota((8, wide))) & (
        sublane_iota((8, wide)) < KVH
    )
    value_mask = value_mask & (sublane_iota((8, wide)) < KVH)
    queue = []
    for slot in range(pages + 1):
        spread = jnp.concatenate(
            [
                jnp.where(
                    key_mask,
                    jnp.broadcast_to(query_ref[member, slot : slot + 1, :], (8, wide)),
                    0.0,
                )
                for member in range(GROUPS)
            ],
            axis=0,
        ).astype(BF16)
        key_rows = page_ref[slot, :, :wide] if slot < pages else fresh_ref[:, :wide]
        queue.append(dot_rows(spread, key_rows))
    for slot, scores in enumerate(queue):
        count = valid_ref[slot : slot + 1, : scores.shape[1]]
        weights = jnp.where(lane_iota(scores.shape) < count, jnp.exp(scores), 0.0)
        queue[slot] = weights.astype(BF16), jnp.sum(weights, axis=1, keepdims=True)
    for slot, (weights, totals) in enumerate(queue):
        if slot < pages:
            value_rows = page_ref[slot, :, ENTRY - wide :]
        else:
            value_rows = fresh_ref[:, ENTRY - wide :]
        queue[slot] = dot(weights, value_rows), totals
    for slot, (weighted, totals) in enumerate(queue):
        for member in range(GROUPS):
            low = member * 8
            kept = jnp.where(value_mask, weighted[low : low + 8], 0.0)
            kept = jnp.where(total_mask, totals[low : low + 8], kept)
            partial_ref[slot * 8 : slot * 8 + 8, member * wide : (member + 1) * wide] = kept

    depth = partial_ref.shape[0]
    spread_row = jnp.sum(
        jnp.where(
            lane_iota((slots, depth)) // 8 == sublane_iota((slots, depth)),
            jnp.broadcast_to(row, (slots, depth)).astype(F32),
            0.0,
        ),
        axis=0,
        keepdims=True,
    ).astype(I32)
    place = sublane_iota((pool_count * 8, depth))
    place = place // 8 * group_rows + place % group_rows
    collect = jnp.where(place == spread_row, 1.0, 0.0).astype(BF16)
    high, low = two_halves(partial_ref[...])
    collected = dot(collect, high) + dot(collect, low)
    summed = [collected[:, member * wide : (member + 1) * wide] for member in range(GROUPS)]
    first = lane_iota((pool_count * 8, LANES)) < KVH
    totals = None
    for member in range(GROUPS):
        moved = move_lanes(jnp.where(first, summed[member][:, :LANES], 0.0), KVH * member)
        totals = moved if totals is None else totals + moved
    rounded = totals.astype(BF16).astype(F32)
    totals = rounded + move_lanes(totals - rounded, H)

    head_cols = H * HD // mp_count
    width = sums_ref.shape[3]

    def sum_tile(key):
        if key == "totals":
            return totals
        member, tile = key
        return summed[member][:, tile * LANES : (tile + 1) * LANES]

    for part in range(mp_count):

        def sum_source(column):
            if column >= head_cols:
                lane = column - head_cols
                return ("totals", lane) if lane < 2 * H else None
            kv, member = divmod((part * head_cols + column) // HD, GROUPS)
            lane = value_skip + kv * HD + (part * head_cols + column) % HD
            return (member, lane // LANES), lane % LANES

        block = jnp.concatenate(
            [lane_tile(sum_tile, start, sum_source) for start in range(0, width, LANES)], axis=1
        )
        block = block.reshape(pool_count, 8, width)[:, :group_rows]
        sums_ref[:, part] = block.astype(BF16)


def mix_kernel(sums_ref, hidden_ref, weight_ref, kept_ref, sent_ref):
    head_cols = weight_ref.shape[0]
    group_rows = hidden_ref.shape[0]
    part = lax.axis_index("mp")
    sums = jnp.sum(sums_ref[...].astype(F32), axis=0)
    tile = head_cols // LANES * LANES
    totals = sums[:, tile : tile + LANES]
    column = lane_iota((LANES, head_cols)) + part * head_cols
    head = column // HD
    lane = sublane_iota((LANES, head_cols)) - (head_cols - tile)
    index = head % GROUPS * KVH + head // GROUPS
    spread = jnp.where((lane == index) | (lane == index + H), 1.0, 0.0).astype(BF16)
    high = totals.astype(BF16)
    middle, low = two_halves(totals - high.astype(F32))
    denominator = dot(high, spread) + dot(middle, spread) + dot(low, spread)
    attended = (sums[:, :head_cols] / denominator).astype(BF16)
    projected = dot(attended, weight_ref[...])
    kept_ref[...] = projected + hidden_ref[...].astype(F32)
    sent_ref[...] = projected.astype(BF16)


def feed_kernel(*refs, steps):
    kept_ref, *arrived = refs[: steps + 1]
    gain_ref, gate_ref, up_ref, down_ref = refs[steps + 1 : steps + 5]
    base_ref, *sent = refs[steps + 5 : 2 * steps + 6]
    part_ref = refs[-1]
    group_rows = kept_ref.shape[0]
    part = lax.axis_index("mp")
    mixed = kept_ref[...]
    for ref in arrived:
        mixed = mixed + ref[...].astype(F32)
    mixed = mixed.astype(BF16).astype(F32)
    normed = rms_scale(mixed, gain_ref[...], EPS_WIDE).astype(BF16)
    gate = dot(normed, gate_ref[...])
    up = dot(normed, up_ref[...])
    hidden = (gate * jax.nn.sigmoid(gate) * up).astype(BF16)
    part_ref[:group_rows] = dot(hidden, down_ref[...])
    own = part_ref[pl.ds(part, 1), :]
    for step, ref in enumerate(sent):
        target = lax.rem(part + (step + 1), steps + 1)
        ref[...] = part_ref[pl.ds(target, 1), :].astype(BF16)
    part_ref[:group_rows] = mixed
    base_ref[...] = own + part_ref[pl.ds(part, 1), :]


def in_vmem(count):
    return [pl.BlockSpec(memory_space=pltpu.VMEM)] * count


def in_hbm(count):
    return [pl.BlockSpec(memory_space=pltpu.HBM)] * count


def params(limit):
    return pltpu.CompilerParams(vmem_limit_bytes=limit * MIB)


def cost(count):
    return pl.CostEstimate(flops=count, bytes_accessed=0, transcendentals=0)


def like(array):
    return jax.ShapeDtypeStruct(array.shape, array.dtype)


def far(*arrays):
    return [pltpu.with_memory_space_constraint(array, pltpu.HBM) for array in arrays]


def room(array):
    return pltpu.VMEM(array.shape, array.dtype)


def shards(
    hidden_in,
    mix_gain,
    project_in,
    query_gain,
    key_gain,
    page_cache,
    page_table,
    lengths,
    row_order,
    out_weight,
    feed_gain,
    gate_weight,
    up_weight,
    down_weight,
):
    pool_count = lax.axis_size("pool")
    mp_count = lax.axis_size("mp")
    devices = pool_count * mp_count
    group_rows, model = hidden_in.shape
    pages = page_cache.shape[0]
    columns = project_in.shape[1]
    padded = up_to(columns, LANES)
    head_cols = H * HD // mp_count
    width = up_to(head_cols + 2 * H, LANES)
    slots = up_to(pages + 1, 8)
    everyone = ("pool", "mp")
    exponent = np.arange(LANES) % (HD // 2) * (-2.0 / HD)
    frequency = jnp.asarray((10000.0**exponent).astype(np.float32)[None])

    operands = (
        hidden_in,
        mix_gain[None],
        project_in.T,
        page_table,
        lengths[None],
        row_order[None],
        frequency,
        query_gain[None],
        key_gain[None],
    )
    table = jax.ShapeDtypeStruct((slots, LANES), F32)
    index = jax.ShapeDtypeStruct((slots, LANES), I32)
    packed, *found = pl.pallas_call(
        lambda *refs: project_kernel(*refs, pages=pages),
        out_shape=(
            jax.ShapeDtypeStruct((devices, group_rows, padded), BF16),
            table,
            table,
            table,
            table,
            index,
            index,
        ),
        in_specs=in_hbm(9),
        out_specs=in_vmem(7),
        scratch_shapes=[room(x) for x in operands] + [pltpu.SemaphoreType.DMA((16,))],
        compiler_params=params(8),
        cost_estimate=cost(10_000_000_000),
        name="project",
    )(*far(*operands))
    packed = lax.all_to_all(packed, everyone, 0, 0, tiled=True)

    wide = up_to(KEYS, LANES)
    sums, new_entries = pl.pallas_call(
        lambda *refs: attend_kernel(
            *refs,
            pool_count=pool_count,
            mp_count=mp_count,
            group_rows=group_rows,
            columns=columns,
        ),
        out_shape=(
            jax.ShapeDtypeStruct((pool_count, mp_count, group_rows, width), BF16),
            jax.ShapeDtypeStruct((1, ENTRY), BF16),
        ),
        in_specs=in_vmem(8),
        out_specs=in_vmem(2),
        scratch_shapes=[
            pltpu.VMEM((GROUPS, slots, wide), F32),
            pltpu.VMEM((16, ENTRY), BF16),
            pltpu.VMEM(((pages + 1) * 8, GROUPS * wide), F32),
        ],
        compiler_params=params(16),
        cost_estimate=cost(20_000_000_000),
        name="attend",
    )(
        packed,
        page_cache,
        *found,
    )
    sums = lax.all_to_all(
        sums.reshape(devices, group_rows, width), everyone, 0, 0, tiled=True
    )

    kept, sent = pl.pallas_call(
        mix_kernel,
        out_shape=(
            jax.ShapeDtypeStruct((group_rows, model), F32),
            jax.ShapeDtypeStruct((group_rows, model), BF16),
        ),
        in_specs=in_vmem(3),
        out_specs=in_vmem(2),
        compiler_params=params(8),
        cost_estimate=cost(20_000_000_000),
        name="mix",
    )(sums, hidden_in, out_weight)

    def ring(value, step):
        return lax.ppermute(value, "mp", [(i, (i + step) % mp_count) for i in range(mp_count)])

    def swap(value, step):
        if mp_count & (mp_count - 1):
            return ring(value, step)
        step ^= step >> 1
        return lax.ppermute(value, "mp", [(i, i ^ step) for i in range(mp_count)])

    steps = mp_count - 1
    arrived = [swap(sent, step) for step in range(1, mp_count)]
    base, *rows = pl.pallas_call(
        lambda *refs: feed_kernel(*refs, steps=steps),
        out_shape=(jax.ShapeDtypeStruct((1, model), F32),)
        + (jax.ShapeDtypeStruct((1, model), BF16),) * steps,
        in_specs=in_vmem(steps + 5),
        out_specs=in_vmem(steps + 1),
        scratch_shapes=[pltpu.VMEM((8, model), F32)],
        compiler_params=params(24),
        name="feed",
    )(kept, *arrived, feed_gain[None], gate_weight, up_weight, down_weight)
    for step, row in enumerate(rows):
        base = base + ring(row, step + 1).astype(F32)
    return (base.astype(BF16), new_entries)


def solution(mesh):
    in_specs = (
        P("pool", None),
        P(),
        P(None, "mp"),
        P(),
        P(),
        P(("pool", "mp"), None, None),
        P(),
        P(),
        P(),
        P("mp", None),
        P(),
        P(None, "mp"),
        P(None, "mp"),
        P("mp", None),
    )
    out_specs = (P(("pool", "mp"), None), P(("pool", "mp"), None))
    return jax.shard_map(shards, mesh=mesh, in_specs=in_specs, out_specs=out_specs, check_vma=False)
```

```python
import jax
import jax.numpy as jnp
import numpy as np
from jax import lax
from jax.experimental import pallas as pl
from jax.experimental.pallas import tpu as pltpu
from jax.sharding import PartitionSpec as P

H = 20
KVH = 5
HD = 64
GROUPS = H // KVH
PAGE = 128
LANES = 128
KEYS = KVH * HD
ENTRY = 2 * KEYS
EPS_WIDE = 1e-05
EPS_HEAD = 1e-06
MIB = 1 << 20

BF16 = jnp.bfloat16
F32 = jnp.float32
I32 = jnp.int32


def up_to(value, step):
    return (value + step - 1) // step * step


def dot(left, right):
    return jnp.dot(left, right, preferred_element_type=F32)


def dot_rows(left, right):
    return lax.dot_general(left, right, (((1,), (1,)), ((), ())), preferred_element_type=F32)


def two_halves(values):
    high = values.astype(BF16)
    return high, (values - high.astype(F32)).astype(BF16)


def lane_iota(shape):
    return lax.broadcasted_iota(I32, shape, len(shape) - 1)


def sublane_iota(shape):
    return lax.broadcasted_iota(I32, shape, len(shape) - 2)


def move_lanes(tile, shift):
    shift %= LANES
    return tile if shift == 0 else pltpu.roll(tile, shift, 1)


def lane_tile(tiles, start, source, step=16):
    spans = []
    for lane in range(0, LANES, step):
        found = source(start + lane)
        piece = None if found is None else (found[0], (lane - found[1]) % LANES)
        if spans and spans[-1][0] == piece:
            spans[-1][2] = lane + step
        else:
            spans.append([piece, lane, lane + step])
    ranges = {}
    for piece, low, high in spans:
        ranges.setdefault(piece, []).append((low, high))
    values = {
        piece: None if piece is None else move_lanes(tiles(piece[0]), piece[1]) for piece in ranges
    }
    like = next(value for value in values.values() if value is not None)
    result = None
    for piece, value in values.items():
        value = jnp.zeros_like(like) if value is None else value
        if result is None:
            result = value
            continue
        lanes = lane_iota(like.shape)
        inside = None
        for low, high in ranges[piece]:
            here = (lanes >= low) & (lanes < high)
            inside = here if inside is None else inside | here
        result = jnp.where(inside, value, result)
    return result


def swap_halves(tile):
    lanes = lane_iota(tile.shape) % HD
    return jnp.where(
        lanes < HD // 2, move_lanes(tile, LANES - HD // 2), move_lanes(tile, HD // 2)
    )


def rms_scale(values, scaling, epsilon):
    mean_square = jnp.mean(values * values, axis=-1, keepdims=True)
    return values * lax.rsqrt(mean_square + epsilon) * scaling


def copy_in(source, target, semaphore):
    copy = pltpu.make_async_copy(source, target, semaphore)
    copy.start()
    return copy


def find_pages(
    table_ref,
    length_ref,
    order_ref,
    frequency_ref,
    query_gain_ref,
    key_gain_ref,
    query_cos_ref,
    query_sin_ref,
    key_cos_ref,
    key_sin_ref,
    row_ref,
    valid_ref,
    pages,
):
    device = lax.axis_index("pool") * lax.axis_size("mp") + lax.axis_index("mp")
    slots = row_ref.shape[0]
    requests, blocks = table_ref.shape
    table = table_ref[...]
    first_page, own_row = device * pages, device
    entry = (sublane_iota(table.shape) * blocks + lane_iota(table.shape) + 1).astype(F32)
    found = [
        jnp.sum(jnp.where(table == first_page + slot, entry, 0.0), axis=0, keepdims=True)
        for slot in range(pages)
    ]
    found.append(jnp.zeros((slots - pages, blocks), F32))
    found = jnp.sum(jnp.concatenate(found, axis=0), axis=1, keepdims=True).astype(I32) - 1
    slot = sublane_iota((slots, 1))
    order = order_ref[...]
    lanes = lane_iota(order.shape)
    own_request = jnp.sum(
        jnp.where(lanes == own_row, order, 0).astype(F32), axis=1, keepdims=True
    ).astype(I32)
    request = jnp.where(slot == pages, own_request, jnp.where(found < 0, -1, found // blocks))
    block = jnp.where(found < 0, 0, found % blocks)
    lane_full = lane_iota((slots, requests))
    length = jnp.sum(
        jnp.where(lane_full == request, length_ref[...].astype(F32), 0.0), axis=1, keepdims=True
    )
    row = jnp.sum(
        jnp.where(order == request, lane_full.astype(F32), 0.0), axis=1, keepdims=True
    ).astype(I32)
    row = jnp.where(request < 0, -1, row)
    valid = jnp.clip(length.astype(I32) - block * PAGE, 0, PAGE)
    valid = jnp.where(slot == pages, 1, jnp.where(request < 0, 0, valid))
    angles = length * frequency_ref[...]
    cosines, sines = jnp.cos(angles), jnp.sin(angles)
    half = lane_iota(angles.shape) % HD
    sines = jnp.where(half < HD // 2, -sines, sines)
    for gain_ref, cos_ref, sin_ref, factor in (
        (query_gain_ref, query_cos_ref, query_sin_ref, HD ** (-0.5)),
        (key_gain_ref, key_cos_ref, key_sin_ref, 1.0),
    ):
        gain = jnp.broadcast_to(gain_ref[...] * factor, (8, HD))
        gain = jnp.concatenate([gain, gain], axis=1)
        cos_ref[...] = cosines * gain[:1]
        sin_ref[...] = sines * swap_halves(gain)[:1]
    row_ref[...] = jnp.broadcast_to(row, row_ref.shape)
    valid_ref[...] = jnp.broadcast_to(valid, valid_ref.shape)


def project_kernel(*refs, pages):
    sources, outputs, rooms, semaphores = refs[:9], refs[9:16], refs[16:25], refs[25]
    rows_ref, gain_ref, weight_ref = rooms[:3]
    out_ref, *found = outputs
    columns = weight_ref.shape[0]
    chunk = up_to(columns // 4, 16)
    first = [copy_in(sources[index], rooms[index], semaphores.at[index]) for index in (0, 1)]
    starts = range(0, columns, chunk)
    copies = []
    for index, start in enumerate(starts):
        part = pl.ds(start, min(chunk, columns - start))
        copies.append(
            copy_in(sources[2].at[part], weight_ref.at[part], semaphores.at[9 + index])
        )
    copies += [
        copy_in(sources[index], rooms[index], semaphores.at[index]) for index in range(3, 9)
    ]
    for copy in first:
        copy.wait()
    normed = rms_scale(rows_ref[...].astype(F32), gain_ref[...], EPS_WIDE).astype(BF16)
    devices, count, padded = out_ref.shape
    if padded > columns:
        out_ref[:, :, columns:] = jnp.zeros((devices, count, padded - columns), BF16)
    for copy in copies:
        copy.wait()
    for start in starts:
        stop = min(start + chunk, columns)
        packed = dot_rows(normed, weight_ref[start:stop])
        out_ref[:, :, start:stop] = jnp.broadcast_to(
            packed.astype(BF16)[None], (devices, count, stop - start)
        )
    find_pages(*rooms[3:], *found, pages)


def attend_kernel(
    packed_ref,
    page_ref,
    query_cos_ref,
    query_sin_ref,
    key_cos_ref,
    key_sin_ref,
    row_ref,
    valid_ref,
    sums_ref,
    entry_ref,
    query_ref,
    fresh_ref,
    partial_ref,
    *,
    pool_count,
    mp_count,
    group_rows,
    columns,
):
    pages = page_ref.shape[0]
    slots = row_ref.shape[0]
    row = row_ref[...][:, :1]
    total_rows = packed_ref.shape[0] * packed_ref.shape[1]
    packed = packed_ref[...].reshape(total_rows, packed_ref.shape[2])
    source = lane_iota((slots, total_rows))
    source_row = source // (mp_count * group_rows) * group_rows + source % group_rows
    source_part = source // group_rows % mp_count
    hit = source_row == row
    choose = jnp.concatenate(
        [jnp.where(hit & (source_part == part), 1.0, 0.0) for part in range(mp_count)], axis=0
    ).astype(BF16)
    chosen = dot(choose, packed)

    def part_tile(key):
        part, tile = key
        return chosen[part * slots : (part + 1) * slots, tile * LANES : (tile + 1) * LANES]

    def part_source(column):
        part, local = divmod(column, columns)
        return (part, local // LANES), local % LANES

    tile_count = (H * HD + ENTRY) // LANES
    query_tiles = H * HD // LANES
    key_tiles = up_to(KEYS, LANES) // LANES
    tiles = [lane_tile(part_tile, t * LANES, part_source) for t in range(tile_count)]
    stacked = jnp.concatenate(tiles[: query_tiles + key_tiles], axis=0)
    ones = jnp.where(
        sublane_iota((2 * LANES, LANES)) % LANES // HD == lane_iota((2 * LANES, LANES)) // HD,
        1.0,
        0.0,
    ).astype(BF16)
    squares = jnp.concatenate(two_halves(stacked * stacked), axis=1)
    scale = lax.rsqrt(dot(squares, ones) * (1.0 / HD) + EPS_HEAD)
    swapped = swap_halves(stacked)
    split = query_tiles * slots

    def turned(low, high, cos_ref, sin_ref):
        shape = ((high - low) // slots, slots, LANES)
        value = stacked[low:high].reshape(shape) * cos_ref[...][None]
        value = value + swapped[low:high].reshape(shape) * sin_ref[...][None]
        return (value * scale[low:high].reshape(shape)).astype(BF16).astype(F32)

    queries = turned(0, split, query_cos_ref, query_sin_ref)
    keys = turned(split, stacked.shape[0], key_cos_ref, key_sin_ref)
    middle = jnp.where(lane_iota((slots, LANES)) < KEYS % LANES, keys[-1], tiles[-key_tiles])
    entries = [keys[t] for t in range(key_tiles - 1)] + [middle] + tiles[-(key_tiles - 1) :]
    fresh = jnp.concatenate(entries, axis=1)[pages : pages + 8]
    entry_ref[...] = fresh[:1].astype(BF16)
    fresh = jnp.where(sublane_iota(fresh.shape) == 0, fresh, 0.0)
    fresh_ref[...] = jnp.concatenate([fresh, jnp.zeros_like(fresh)], axis=0).astype(BF16)

    wide = key_tiles * LANES
    for member in range(GROUPS):

        def query_source(column):
            kv = column // HD
            if kv >= KVH:
                return None
            head = kv * GROUPS + member
            return head // 2, head % 2 * HD + column % HD

        query_ref[member] = jnp.concatenate(
            [
                lane_tile(lambda t: queries[t], t * LANES, query_source)
                for t in range(key_tiles)
            ],
            axis=1,
        )

    key_mask = lane_iota((8, wide)) // HD == sublane_iota((8, wide))
    value_skip = wide - KEYS
    value_mask = (lane_iota((8, wide)) + (HD - value_skip)) // HD == sublane_iota((8, wide)) + 1
    total_mask = (lane_iota((8, wide)) == sublane_iota((8, wide))) & (
        sublane_iota((8, wide)) < KVH
    )
    value_mask = value_mask & (sublane_iota((8, wide)) < KVH)
    queue = []
    for slot in range(pages + 1):
        spread = jnp.concatenate(
            [
                jnp.where(
                    key_mask,
                    jnp.broadcast_to(query_ref[member, slot : slot + 1, :], (8, wide)),
                    0.0,
                )
                for member in range(GROUPS)
            ],
            axis=0,
        ).astype(BF16)
        key_rows = page_ref[slot, :, :wide] if slot < pages else fresh_ref[:, :wide]
        queue.append(dot_rows(spread, key_rows))
    for slot, scores in enumerate(queue):
        count = valid_ref[slot : slot + 1, : scores.shape[1]]
        weights = jnp.where(lane_iota(scores.shape) < count, jnp.exp(scores), 0.0)
        queue[slot] = weights.astype(BF16), jnp.sum(weights, axis=1, keepdims=True)
    for slot, (weights, totals) in enumerate(queue):
        if slot < pages:
            value_rows = page_ref[slot, :, ENTRY - wide :]
        else:
            value_rows = fresh_ref[:, ENTRY - wide :]
        queue[slot] = dot(weights, value_rows), totals
    for slot, (weighted, totals) in enumerate(queue):
        for member in range(GROUPS):
            low = member * 8
            kept = jnp.where(value_mask, weighted[low : low + 8], 0.0)
            kept = jnp.where(total_mask, totals[low : low + 8], kept)
            partial_ref[slot * 8 : slot * 8 + 8, member * wide : (member + 1) * wide] = kept

    depth = partial_ref.shape[0]
    spread_row = jnp.sum(
        jnp.where(
            lane_iota((slots, depth)) // 8 == sublane_iota((slots, depth)),
            jnp.broadcast_to(row, (slots, depth)).astype(F32),
            0.0,
        ),
        axis=0,
        keepdims=True,
    ).astype(I32)
    place = sublane_iota((pool_count * 8, depth))
    place = place // 8 * group_rows + place % group_rows
    collect = jnp.where(place == spread_row, 1.0, 0.0).astype(BF16)
    high, low = two_halves(partial_ref[...])
    collected = dot(collect, high) + dot(collect, low)
    summed = [collected[:, member * wide : (member + 1) * wide] for member in range(GROUPS)]
    first = lane_iota((pool_count * 8, LANES)) < KVH
    totals = None
    for member in range(GROUPS):
        moved = move_lanes(jnp.where(first, summed[member][:, :LANES], 0.0), KVH * member)
        totals = moved if totals is None else totals + moved
    rounded = totals.astype(BF16).astype(F32)
    totals = rounded + move_lanes(totals - rounded, H)

    head_cols = H * HD // mp_count
    width = sums_ref.shape[3]

    def sum_tile(key):
        if key == "totals":
            return totals
        member, tile = key
        return summed[member][:, tile * LANES : (tile + 1) * LANES]

    for part in range(mp_count):

        def sum_source(column):
            if column >= head_cols:
                lane = column - head_cols
                return ("totals", lane) if lane < 2 * H else None
            kv, member = divmod((part * head_cols + column) // HD, GROUPS)
            lane = value_skip + kv * HD + (part * head_cols + column) % HD
            return (member, lane // LANES), lane % LANES

        block = jnp.concatenate(
            [lane_tile(sum_tile, start, sum_source) for start in range(0, width, LANES)], axis=1
        )
        block = block.reshape(pool_count, 8, width)[:, :group_rows]
        sums_ref[:, part] = block.astype(BF16)


def mix_kernel(sums_ref, hidden_ref, weight_ref, kept_ref, sent_ref):
    head_cols = weight_ref.shape[0]
    group_rows = hidden_ref.shape[0]
    part = lax.axis_index("mp")
    sums = jnp.sum(sums_ref[...].astype(F32), axis=0)
    tile = head_cols // LANES * LANES
    totals = sums[:, tile : tile + LANES]
    column = lane_iota((LANES, head_cols)) + part * head_cols
    head = column // HD
    lane = sublane_iota((LANES, head_cols)) - (head_cols - tile)
    index = head % GROUPS * KVH + head // GROUPS
    spread = jnp.where((lane == index) | (lane == index + H), 1.0, 0.0).astype(BF16)
    high = totals.astype(BF16)
    middle, low = two_halves(totals - high.astype(F32))
    terms = jnp.concatenate([high, middle, low], axis=1)
    denominator = dot(terms, jnp.concatenate([spread] * 3, axis=0))
    attended = (sums[:, :head_cols] / denominator).astype(BF16)
    projected = dot(attended, weight_ref[...])
    kept_ref[...] = projected + hidden_ref[...].astype(F32)
    sent_ref[...] = projected.astype(BF16)


def feed_kernel(*refs, steps):
    kept_ref, *arrived = refs[: steps + 1]
    gain_ref, gate_ref, up_ref, down_ref = refs[steps + 1 : steps + 5]
    base_ref, *sent = refs[steps + 5 : 2 * steps + 6]
    part_ref = refs[-1]
    group_rows = kept_ref.shape[0]
    part = lax.axis_index("mp")
    mixed = kept_ref[...]
    for ref in arrived:
        mixed = mixed + ref[...].astype(F32)
    mixed = mixed.astype(BF16).astype(F32)
    normed = rms_scale(mixed, gain_ref[...], EPS_WIDE).astype(BF16)
    gate = dot(normed, gate_ref[...])
    up = dot(normed, up_ref[...])
    hidden = (gate * jax.nn.sigmoid(gate) * up).astype(BF16)
    part_ref[:group_rows] = dot(hidden, down_ref[...])
    own = part_ref[pl.ds(part, 1), :]
    for step, ref in enumerate(sent):
        target = lax.rem(part + (step + 1), steps + 1)
        ref[...] = part_ref[pl.ds(target, 1), :].astype(BF16)
    part_ref[:group_rows] = mixed
    base_ref[...] = own + part_ref[pl.ds(part, 1), :]


def in_vmem(count):
    return [pl.BlockSpec(memory_space=pltpu.VMEM)] * count


def in_hbm(count):
    return [pl.BlockSpec(memory_space=pltpu.HBM)] * count


def params(limit):
    return pltpu.CompilerParams(vmem_limit_bytes=limit * MIB)


def cost(count):
    return pl.CostEstimate(flops=count, bytes_accessed=0, transcendentals=0)


def like(array):
    return jax.ShapeDtypeStruct(array.shape, array.dtype)


def far(*arrays):
    return [pltpu.with_memory_space_constraint(array, pltpu.HBM) for array in arrays]


def room(array):
    return pltpu.VMEM(array.shape, array.dtype)


def shards(
    hidden_in,
    mix_gain,
    project_in,
    query_gain,
    key_gain,
    page_cache,
    page_table,
    lengths,
    row_order,
    out_weight,
    feed_gain,
    gate_weight,
    up_weight,
    down_weight,
):
    pool_count = lax.axis_size("pool")
    mp_count = lax.axis_size("mp")
    devices = pool_count * mp_count
    group_rows, model = hidden_in.shape
    pages = page_cache.shape[0]
    columns = project_in.shape[1]
    padded = up_to(columns, LANES)
    head_cols = H * HD // mp_count
    width = up_to(head_cols + 2 * H, LANES)
    slots = up_to(pages + 1, 8)
    everyone = ("pool", "mp")
    exponent = np.arange(LANES) % (HD // 2) * (-2.0 / HD)
    frequency = jnp.asarray((10000.0**exponent).astype(np.float32)[None])

    operands = (
        hidden_in,
        mix_gain[None],
        project_in.T,
        page_table,
        lengths[None],
        row_order[None],
        frequency,
        query_gain[None],
        key_gain[None],
    )
    table = jax.ShapeDtypeStruct((slots, LANES), F32)
    index = jax.ShapeDtypeStruct((slots, LANES), I32)
    packed, *found = pl.pallas_call(
        lambda *refs: project_kernel(*refs, pages=pages),
        out_shape=(
            jax.ShapeDtypeStruct((devices, group_rows, padded), BF16),
            table,
            table,
            table,
            table,
            index,
            index,
        ),
        in_specs=in_hbm(9),
        out_specs=in_vmem(7),
        scratch_shapes=[room(x) for x in operands] + [pltpu.SemaphoreType.DMA((16,))],
        compiler_params=params(8),
        cost_estimate=cost(10_000_000_000),
        name="project",
    )(*far(*operands))
    packed = lax.all_to_all(packed, everyone, 0, 0, tiled=True)

    wide = up_to(KEYS, LANES)
    sums, new_entries = pl.pallas_call(
        lambda *refs: attend_kernel(
            *refs,
            pool_count=pool_count,
            mp_count=mp_count,
            group_rows=group_rows,
            columns=columns,
        ),
        out_shape=(
            jax.ShapeDtypeStruct((pool_count, mp_count, group_rows, width), BF16),
            jax.ShapeDtypeStruct((1, ENTRY), BF16),
        ),
        in_specs=in_vmem(8),
        out_specs=in_vmem(2),
        scratch_shapes=[
            pltpu.VMEM((GROUPS, slots, wide), F32),
            pltpu.VMEM((16, ENTRY), BF16),
            pltpu.VMEM(((pages + 1) * 8, GROUPS * wide), F32),
        ],
        compiler_params=params(16),
        cost_estimate=cost(20_000_000_000),
        name="attend",
    )(
        packed,
        page_cache,
        *found,
    )
    sums = lax.all_to_all(
        sums.reshape(devices, group_rows, width), everyone, 0, 0, tiled=True
    )

    kept, sent = pl.pallas_call(
        mix_kernel,
        out_shape=(
            jax.ShapeDtypeStruct((group_rows, model), F32),
            jax.ShapeDtypeStruct((group_rows, model), BF16),
        ),
        in_specs=in_vmem(3),
        out_specs=in_vmem(2),
        compiler_params=params(8),
        cost_estimate=cost(20_000_000_000),
        name="mix",
    )(sums, hidden_in, out_weight)

    def ring(value, step):
        return lax.ppermute(value, "mp", [(i, (i + step) % mp_count) for i in range(mp_count)])

    def swap(value, step):
        if mp_count & (mp_count - 1):
            return ring(value, step)
        step ^= step >> 1
        return lax.ppermute(value, "mp", [(i, i ^ step) for i in range(mp_count)])

    steps = mp_count - 1
    arrived = [swap(sent, step) for step in range(1, mp_count)]
    base, *rows = pl.pallas_call(
        lambda *refs: feed_kernel(*refs, steps=steps),
        out_shape=(jax.ShapeDtypeStruct((1, model), F32),)
        + (jax.ShapeDtypeStruct((1, model), BF16),) * steps,
        in_specs=in_vmem(steps + 5),
        out_specs=in_vmem(steps + 1),
        scratch_shapes=[pltpu.VMEM((8, model), F32)],
        compiler_params=params(24),
        name="feed",
    )(kept, *arrived, feed_gain[None], gate_weight, up_weight, down_weight)
    for step, row in enumerate(rows):
        base = base + ring(row, step + 1).astype(F32)
    return (base.astype(BF16), new_entries)


def solution(mesh):
    in_specs = (
        P("pool", None),
        P(),
        P(None, "mp"),
        P(),
        P(),
        P(("pool", "mp"), None, None),
        P(),
        P(),
        P(),
        P("mp", None),
        P(),
        P(None, "mp"),
        P(None, "mp"),
        P("mp", None),
    )
    out_specs = (P(("pool", "mp"), None), P(("pool", "mp"), None))
    return jax.shard_map(shards, mesh=mesh, in_specs=in_specs, out_specs=out_specs, check_vma=False)
```
